256 devices in a mesh: section: 16 (over y, x_hi, core), expert: 16 (over z, x_lo).
Axes of the slice: x: 4 (x_hi: 2, x_lo: 2; x = x_hi * 2 + x_lo), y: 4, z: 8, core: 2. Of those that a mesh axis runs over, the one named last changes fastest.
Arguments:
- grad_out: bfloat16 [16, 2048, 1024], P('section', 'expert'), may hold values from -6 to 6
- saved_inputs: bfloat16 [16, 2, 2048, 1024], P('section', None, 'expert'), may hold values from -6 to 6
- routes: int32 [16, 2, 2048, 8], P('section', None, 'expert'), may hold values from 0 to 31, all different within a row; in each aligned block of 128 rows (0 to 127, 128 to 255, ..., all dimensions but the last counted through in order) at most 40 rows name the same one
- gate_weights: float32 [16, 2, 2048, 8], P('section', None, 'expert'), may hold values from 0.05 to 0.3
- w_gate: bfloat16 [16, 32, 1024, 512], P('section', 'expert'), may hold values from -0.1875 to 0.1875
- w_up: bfloat16 [16, 32, 1024, 512], P('section', 'expert'), may hold values from -0.1875 to 0.1875
- w_down: bfloat16 [16, 32, 512, 1024], P('section', 'expert'), may hold values from -0.25 to 0.25
Outputs:
- input_grad: bfloat16 [16, 2048, 1024], P('section', 'expert')
The draws below stay inside these ranges and needn't reach their ends.
Inputs may be any that keep to these rules, and one draw needn't show every extreme that they name: `routes`: each row names 8 different experts. In the rows of one device at one step (aligned blocks of 128 rows) no expert is named by more than 40 rows; in some blocks one expert is named by exactly 40.
All inputs are finite; a program needn't handle non-finite values.
Results may differ from the reference program's by a relative error of at most 0.007.
Values may be sent and summed in bfloat16 or wider, within the bound.
A program may use at most 64 MiB of HBM per device.

```python
import math
import jax
import jax.numpy as jnp
import numpy as np
from jax import lax

D = 1024
H = 512
EXPERTS = 32
TOP = 8
TOK_DEV = 128
TICKS = 2
MOST = 40
TOKENS = 2048
SECTIONS = 16
N_EXPERT = 16


def level_of(key, shape, pieces, smallest, high):
    def one(dim, blocks):
        heights = jax.random.uniform(jax.random.fold_in(jax.random.fold_in(key, 6), dim), (blocks,), jnp.float32, smallest / len(pieces), high / len(pieces))
        return jnp.repeat(jnp.exp(heights), shape[dim] // blocks).reshape((-1,) + (1,) * (len(shape) - dim - 1))

    loudness = one(*pieces[0])
    for cut in pieces[1:]:
        loudness = loudness * one(*cut)
    return loudness


def assign_block(own_key, own, number, rows, count, top, bound, skew):
    sequence = jax.random.permutation(own_key, count)
    heavy_load, ordinary = portions_of(count, rows * top, bound, skew, True), portions_of(count, rows * top, bound, skew, False)
    places = jnp.arange(count)

    def named(lengths, rotation):
        used = int((lengths > 0).sum())
        fixed = max(1, used // 4)
        moved = fixed + (places - fixed + rotation * (used - fixed)) % max(1, count - fixed)
        return jnp.zeros((count,), jnp.int32).at[sequence[jnp.where(places < fixed, places, moved)]].set(jnp.asarray(lengths, jnp.int32))

    lengths = jnp.where(number % 4 == 0, named(heavy_load, number // 4), named(ordinary, number - number // 4 - 1))
    mixed = jax.random.permutation(jax.random.fold_in(own, 3), count)
    source_of, taker = mixed[0:count // 2 * 2:2], mixed[1:count // 2 * 2:2]
    slack = jnp.minimum(lengths[source_of] - 1, bound - lengths[taker]) // 2
    slack = jnp.where((source_of == sequence[0]) | (taker == sequence[0]) | (lengths[taker] == 0), 0, jnp.maximum(slack, 0))
    moved = jax.random.randint(jax.random.fold_in(own, 4), (count // 2,), 0, 1 << 20) % (slack + 1)
    lengths = lengths.at[source_of].add(-moved).at[taker].add(moved)
    labels = jnp.searchsorted(jnp.cumsum(lengths), jnp.arange(rows * top), side="right").astype(jnp.int32)
    table = labels.reshape(top, rows).T
    table = table[jax.random.permutation(jax.random.fold_in(own, 1), rows)]
    rotation = jax.random.randint(jax.random.fold_in(own, 2), (rows, 1), 0, top)
    return jnp.take_along_axis(table, (jnp.arange(top)[None, :] + rotation) % top, axis=1)


def portions_of(count, total, limit, lean, full):
    portions = [(1 << 20) // math.isqrt(standing ** lean) + 1 for standing in range(1, count + 1)]
    largest = limit if full else min(limit, max(-(-total // count), total * portions[0] // sum(portions)))
    least = 1 if total - largest >= count - 1 else 0
    counts, spare = [largest] + [least] * (count - 1), total - largest - least * (count - 1)
    while spare > 0:
        candidates = [i for i in range(1, count) if counts[i] < largest] or [i for i in range(1, count) if counts[i] < limit]
        whole, left = sum([portions[i] for i in candidates]), spare
        for i in candidates:
            addition = min(limit - counts[i], max(1, left * portions[i] // whole), spare)
            counts[i] = counts[i] + addition
            spare = spare - addition
    return np.array(counts)


def scatter_about(own_key, shape, spread, most, cuts=(), kind=jnp.bfloat16):
    level = level_of(own_key, shape, cuts, -0.22, 0.18) if cuts else 1.0
    entries = jax.random.normal(own_key, shape, jnp.float32) * spread * level
    return jnp.minimum(jnp.maximum(entries, -most), most).astype(kind)


def setup_inputs(seed: int = 0) -> dict:
    seeds = jax.random.split(jax.random.key(seed), 8)
    grad_out = scatter_about(seeds[0], (SECTIONS, TOKENS, D), 1.0, 6.0, ((0, 16), (1, 16)))
    saved_inputs = scatter_about(seeds[1], (SECTIONS, TICKS, TOKENS, D), 1.0, 6.0, ((0, 16), (2, 16)))
    routes_keys = jax.random.split(jax.random.fold_in(seeds[2], 1), SECTIONS * TICKS * TOKENS // TOK_DEV)
    routes_turns = jax.random.permutation(jax.random.fold_in(seeds[2], 3), SECTIONS * TICKS * TOKENS // TOK_DEV)
    routes = jax.vmap(lambda own, number: assign_block(jax.random.fold_in(seeds[2], 2), own, number, TOK_DEV, EXPERTS, TOP, MOST, 2))(routes_keys, routes_turns).reshape((SECTIONS, TICKS, TOKENS, TOP))
    gate_weights = jnp.clip(0.05 + 0.25 * jax.random.uniform(seeds[3], (SECTIONS, TICKS, TOKENS, TOP), jnp.float32) ** level_of(seeds[3], (SECTIONS, TICKS, TOKENS, TOP), ((0, 16), (2, 16)), -0.2, 0.2), 0.05, 0.3)
    w_gate = scatter_about(seeds[4], (SECTIONS, EXPERTS, D, H), D ** -0.5, 0.1875, ((0, 16), (1, 16)))
    w_up = scatter_about(seeds[5], (SECTIONS, EXPERTS, D, H), D ** -0.5, 0.1875, ((0, 16), (1, 16)))
    w_down = scatter_about(seeds[6], (SECTIONS, EXPERTS, H, D), H ** -0.5, 0.25, ((0, 16), (1, 16)))
    return dict(grad_out=grad_out, saved_inputs=saved_inputs, routes=routes, gate_weights=gate_weights, w_gate=w_gate, w_up=w_up, w_down=w_down)


def expert_rows(input_rows, grad_rows, gate_proj, up_proj, down_proj):
    inputs_f = input_rows.astype(jnp.float32)
    gate_pre = jnp.einsum("emd,edh->emh", inputs_f, gate_proj.astype(jnp.float32))
    up_pre = jnp.einsum("emd,edh->emh", inputs_f, up_proj.astype(jnp.float32))
    hidden_grad = jnp.einsum("emd,ehd->emh", grad_rows.astype(jnp.float32), down_proj.astype(jnp.float32))
    sigmoid_gate = jax.nn.sigmoid(gate_pre)
    gate_grad = (hidden_grad * up_pre * sigmoid_gate * (1.0 + gate_pre * (1.0 - sigmoid_gate))).astype(jnp.bfloat16)
    up_grad = (hidden_grad * gate_pre * sigmoid_gate).astype(jnp.bfloat16)
    row_grad = jnp.einsum("emh,edh->emd", gate_grad.astype(jnp.float32), gate_proj.astype(jnp.float32))
    row_grad = row_grad + jnp.einsum("emh,edh->emd", up_grad.astype(jnp.float32), up_proj.astype(jnp.float32))
    return row_grad.astype(jnp.bfloat16)


def section_step(operands):
    grad, saved, route_ids, weights, gate_proj, up_proj, down_proj = operands
    row_total = TOKENS * TOP
    flat_routes = route_ids.reshape(-1).astype(jnp.int32)
    one_hot = (flat_routes[:, None] == jnp.arange(EXPERTS, dtype=jnp.int32)[None, :]).astype(jnp.int32)
    blocks = one_hot.reshape(N_EXPERT, TOK_DEV * TOP, EXPERTS)
    earlier = jnp.cumsum(blocks, axis=1) - blocks
    position = jnp.sum(earlier * blocks, axis=2).reshape(-1)
    owner_rank = jnp.arange(row_total, dtype=jnp.int32) // (TOK_DEV * TOP)
    capacity = N_EXPERT * MOST
    slot_index = flat_routes * capacity + owner_rank * MOST + position
    token_index = jnp.arange(row_total, dtype=jnp.int32) // TOP
    slot_token = jnp.zeros((EXPERTS * capacity,), jnp.int32).at[slot_index].set(token_index)
    slot_live = jnp.zeros((EXPERTS * capacity,), jnp.int32).at[slot_index].set(1)
    input_rows = jnp.where(slot_live[:, None] == 1, saved[slot_token], jnp.zeros((), saved.dtype))
    grad_rows = jnp.where(slot_live[:, None] == 1, grad[slot_token], jnp.zeros((), grad.dtype))
    row_grad = expert_rows(input_rows.reshape(EXPERTS, capacity, D), grad_rows.reshape(EXPERTS, capacity, D), gate_proj, up_proj, down_proj)
    back_rows = row_grad.reshape(EXPERTS * capacity, D)[slot_index].reshape(TOKENS, TOP, D)
    total = grad.astype(jnp.float32) + jnp.sum(weights[:, :, None].astype(jnp.float32) * back_rows.astype(jnp.float32), axis=1)
    return total.astype(jnp.bfloat16)


def reference(grad_out, saved_inputs, routes, gate_weights, w_gate, w_up, w_down):
    grad = grad_out
    result = grad_out
    for step_index in range(TICKS):
        result = lax.map(section_step, (grad, saved_inputs[:, step_index], routes[:, step_index], gate_weights[:, step_index], w_gate, w_up, w_down))
        if step_index + 1 < TICKS:
            grad = jnp.roll(result, -1, axis=0)
    return result
```

```python
import jax
import jax.numpy as jnp
from jax import lax
from jax.experimental import pallas as pl
from jax.experimental.pallas import tpu as pltpu
from jax.sharding import PartitionSpec as P

BF = jnp.bfloat16
F32 = jnp.float32
TOK = 128
D = 1024
H = 512
CAP = 80
RING = 8
PLACE = {0: 0, 1: 1, 7: 2, 2: 3, 6: 4, 3: 5, 5: 6, 4: 7}
SEMS = 224


def nt(a, b):
    return lax.dot_general(a, b, (((1,), (1,)), ((), ())), preferred_element_type=F32)


def nn(a, b):
    return lax.dot_general(a, b, (((1,), (0,)), ((), ())), preferred_element_type=F32)


def kernel(
    grad_in, saved_in, table_in, wg_in, wu_in, wd_in, out_ref,
    g0, x0, x1, g1, tab, wg, wu, wd, part, l_core, l_down, l_up, tot, fin,
    xg, gg, gp, up, rw, ws, pos, post, ssem, rsem, lsem,
):
    s = lax.axis_index("section")
    e = lax.axis_index("expert")
    core = lax.rem(s, 2)
    x_lo = lax.rem(e, 2)
    mixed = core != x_lo
    other_core = s + 1 - 2 * core
    other_x = e + 1 - 2 * x_lo
    z_up = (s, lax.rem(e + 2, 16))
    z_down = (s, lax.rem(e + 14, 16))
    mate = (other_core, e)
    swap = (other_core, other_x)
    pass_to = (lax.rem(s + 16 - 2 * (1 - x_lo), 16), other_x)
    pass_from = (lax.rem(s + 2 * x_lo, 16), other_x)
    home = lax.select(mixed, other_x, e)

    barrier = pltpu.get_barrier_semaphore()
    for peer in (z_up, z_down, mate, swap, pass_to, pass_from):
        pl.semaphore_signal(barrier, inc=1, device_id=peer, device_id_type=pl.DeviceIdType.MESH)

    count = [0]
    sent = {}

    def make(src, dst, peer):
        i = count[0]
        count[0] += 1
        return pltpu.make_async_remote_copy(
            src_ref=src, dst_ref=dst, send_sem=ssem.at[i], recv_sem=rsem.at[i],
            device_id=peer, device_id_type=pl.DeviceIdType.MESH,
        )

    def send(key, src, dst, peer):
        copy = make(src, dst, peer)
        copy.start()
        sent[key] = copy

    moves = {}

    def enter(key, src, dst):
        i = len(moves)
        moves[key] = (pltpu.make_async_copy(src, dst, lsem.at[i]), make(src, dst, swap))

        @pl.when(jnp.logical_not(mixed))
        def _():
            moves[key][0].start()

        @pl.when(mixed)
        def _():
            moves[key][1].start()

    def entered(key):
        @pl.when(jnp.logical_not(mixed))
        def _():
            moves[key][0].wait()

        @pl.when(mixed)
        def _():
            moves[key][1].wait_recv()

    pl.semaphore_wait(barrier, 6)
    enter("t", table_in, tab.at[0, 0])
    enter("x0", saved_in.at[0], x0.at[0, 0])
    enter("g0", grad_in, g0.at[0, 0])
    for j in range(2):
        enter(("wg", j), wg_in.at[j], wg.at[j])
        enter(("wu", j), wu_in.at[j], wu.at[j])
        enter(("wd", j), wd_in.at[j], wd.at[j])
        if j == 0:
            enter("x1", saved_in.at[1], x1.at[0, 0])

    def rows(ch):
        return pl.ds(64 * ch, 64)

    def to_mate(name, buf, d, ch):
        k = PLACE[d]
        send((name, "c", d, ch), buf.at[k, 0, rows(ch)], buf.at[k, 1, rows(ch)], mate)

    def hop(name, buf, way, d, ch):
        src, dst = (d, d + 1) if way == "u" else ((8 - d) % 8, 7 - d)
        send(
            (name, way, d, ch), buf.at[PLACE[src], 0, rows(ch)], buf.at[PLACE[dst], 0, rows(ch)],
            z_up if way == "u" else z_down,
        )

    def gather_first(name, buf, ch):
        hop(name, buf, "u", 0, ch)
        hop(name, buf, "d", 0, ch)
        to_mate(name, buf, 0, ch)

    def gather_step(names, d):
        for ch in range(2):
            for name, buf in names:
                for way in "ud":
                    here = d if way == "u" else 8 - d
                    if d < 4 or (way == "u") == (ch == 0):
                        sent[name, way, d - 1, ch].wait_recv()
                        if d < 3 or (d == 3 and (way == "u") == (ch == 0)):
                            hop(name, buf, way, d, ch)
                        to_mate(name, buf, here, ch)

    def gathered(name, d):
        for ch in range(2):
            sent[name, "c", d, ch].wait_recv()

    def table_step(d):
        if d == 0:
            send(("t", "u", 0), tab.at[0, 0], tab.at[PLACE[1], 0], z_up)
            send(("t", "d", 0), tab.at[0, 0], tab.at[PLACE[7], 0], z_down)
            send(("t", "c", 0), tab.at[0, 0], tab.at[0, 1], mate)
            return
        sent["t", "u", d - 1].wait_recv()
        k = PLACE[d]
        if d < 4:
            send(("t", "u", d), tab.at[k, 0], tab.at[PLACE[d + 1], 0], z_up)
        send(("t", "c", d), tab.at[k, 0], tab.at[k, 1], mate)
        if d < 4:
            sent["t", "d", d - 1].wait_recv()
            k = PLACE[8 - d]
            if d < 3:
                send(("t", "d", d), tab.at[k, 0], tab.at[PLACE[7 - d], 0], z_down)
            send(("t", "c", 8 - d), tab.at[k, 0], tab.at[k, 1], mate)

    def places(t):
        masks = []
        for k in range(RING):
            named = jnp.concatenate([tab[k, 0, t, 0:8], tab[k, 1, t, 0:8]], axis=1)
            for j in range(2):
                hit = named == (2 * home + j).astype(F32)
                masks.append(jnp.sum(jnp.where(hit, 1.0, 0.0), axis=0, keepdims=True))
        mask = jnp.concatenate(masks, axis=0)
        before = lax.broadcasted_iota(jnp.int32, (256, 256), 0) < lax.broadcasted_iota(
            jnp.int32, (256, 256), 1
        )
        earlier = nn(mask.astype(BF), jnp.where(before, 1.0, 0.0).astype(BF))
        where = jnp.where(mask > 0.5, earlier, -1000.0)
        pos[t] = where
        turned = jnp.transpose(jnp.concatenate([where, jnp.zeros((112, 256), F32)], axis=0))
        for k in range(RING):
            post[t, k] = turned[:, 2 * k : 2 * k + 2]

    def chosen(t, k):
        slot = lax.broadcasted_iota(jnp.int32, (CAP, 256), 0).astype(F32)
        return [slot == pos[t, pl.ds(2 * k + j, 1)] for j in range(2)]

    def pick(t, src, dst, k):
        hot = jnp.concatenate([jnp.where(h, 1.0, 0.0) for h in chosen(t, k)], axis=0).astype(BF)
        got = nn(hot, src[k].reshape(256, D)).astype(BF)
        at = pl.ds(pl.multiple_of(k * CAP, 16), CAP)
        dst[0, at] = got[:CAP]
        dst[1, at] = got[CAP:]

    def pick_scales(t, k):
        named = jnp.concatenate([tab[k, 0, t, 0:8], tab[k, 1, t, 0:8]], axis=1)
        weight = jnp.concatenate([tab[k, 0, t, 8:16], tab[k, 1, t, 8:16]], axis=1)
        at = pl.ds(pl.multiple_of(k * CAP, 16), CAP)
        for j, h in enumerate(chosen(t, k)):
            mine = jnp.sum(
                jnp.where(named == (2 * home + j).astype(F32), weight, 0.0), axis=0, keepdims=True
            )
            ws[j, at] = jnp.sum(jnp.where(h, mine, 0.0), axis=1, keepdims=True)

    def pre(j, k0, n):
        at = pl.ds(k0 * CAP, n * CAP)
        x = xg[j, at]
        gp[j, at] = nn(x, wg[j])
        up[j, at] = nn(x, wu[j])

    def post_rows(j, k0, n):
        at = pl.ds(k0 * CAP, n * CAP)
        hidden = nt(gg[j, at], wd[j])
        gate = gp[j, at]
        sig = 1.0 / (1.0 + jnp.exp(-gate))
        hs = hidden * sig
        gate_grad = (hs * up[j, at] * (1.0 + gate * (1.0 - sig))).astype(BF)
        up_grad = (hs * gate).astype(BF)
        grown = nt(gate_grad, wg[j]) + nt(up_grad, wu[j])
        grown = (grown * ws[j, at]).astype(BF)
        for i in range(n):
            rw[k0 + i, j * CAP : (j + 1) * CAP] = grown[i * CAP : (i + 1) * CAP]

    def put(t, k):
        lane = lax.broadcasted_iota(jnp.int32, (256, 2 * CAP), 1).astype(F32)
        col = post[t, k]
        hot = jnp.logical_or(lane == col[:, 0:1], lane == col[:, 1:2] + float(CAP))
        summed = nn(jnp.where(hot, 1.0, 0.0).astype(BF), rw[k])
        part[t, k] = summed.astype(BF).reshape(2, TOK, D)

    def give_mate(t, d):
        k = PLACE[d]
        send((t, "rc", d), part.at[t, k, 1], l_core.at[t, k], mate)

    def give(t, way, d, ch):
        src = PLACE[d]
        if way == "d":
            send((t, "rd", d, ch), part.at[t, src, 0, rows(ch)], l_down.at[t, d - 1, rows(ch)], z_down)
        else:
            i = 7 - d
            send((t, "ru", d, ch), part.at[t, src, 0, rows(ch)], l_up.at[t, i, rows(ch)], z_up)

    def add_up(t, way, d, ch, arrived):
        k = PLACE[d]
        value = part[t, k, 0, rows(ch)].astype(F32) + l_core[t, k, rows(ch)].astype(F32)
        if arrived:
            landed = l_down[t, d, rows(ch)] if way == "d" else l_up[t, 8 - d, rows(ch)]
            value = value + landed.astype(F32)
        part[t, k, 0, rows(ch)] = value.astype(BF)

    def scatter_far(t):
        sent[t, "rc", 4].wait_recv()
        for way, ch in (("d", 0), ("u", 1)):
            add_up(t, way, 4, ch, False)
            give(t, way, 4, ch)

    def scatter_open(t):
        for way, d, ch in (("d", 3, 1), ("u", 5, 0)):
            sent[t, "rc", d].wait_recv()
            add_up(t, way, d, ch, False)
            give(t, way, d, ch)

    def scatter_step(t, n):
        turns = ((0, 1),) if n == 3 else ((1, 0), (0, 1))
        if n != 3:
            sent[t, "rc", n].wait_recv()
            sent[t, "rc", 8 - n].wait_recv()
        for ch_d, ch_u in turns:
            for way, d, ch in (("d", n, ch_d), ("u", 8 - n, ch_u)):
                back = d + 1 if way == "d" else d - 1
                sent[t, "r" + way, back, ch].wait_recv()
                add_up(t, way, d, ch, True)
                give(t, way, d, ch)

    def scatter_last(t, ch, own):
        sent[t, "rd", 1, ch].wait_recv()
        sent[t, "ru", 7, ch].wait_recv()
        at = rows(ch)
        return (
            own[0, 0, at].astype(F32)
            + (part[t, 0, 0, at].astype(F32) + l_core[t, 0, at].astype(F32))
            + (l_down[t, 0, at].astype(F32) + l_up[t, 0, at].astype(F32))
        ).astype(BF)

    def each(body):
        def step(k, carry):
            body(k)
            return carry

        lax.fori_loop(0, RING, step, 0)

    entered("t")
    table_step(0)
    entered("x0")
    for ch in range(2):
        gather_first("x0", x0, ch)
    entered("g0")
    for ch in range(2):
        gather_first("g0", g0, ch)
    first = (("x0", x0), ("g0", g0))
    for d in (1, 2, 3, 4):
        table_step(d)
        gather_step(first, d)
        if d == 3:
            entered("x1")
            for ch in range(2):
                gather_first("x1", x1, ch)
    for d in range(RING):
        sent["t", "c", d].wait_recv()
        gathered("x0", d)
        gathered("g0", d)
    second = (("x1", x1),)
    gather_step(second, 1)
    places(0)
    places(1)

    def pick0(k):
        pick(0, x0, xg, k)
        pick(0, g0, gg, k)
        pick_scales(0, k)

    each(pick0)
    gather_step(second, 2)
    for w in ("wg", "wu", "wd"):
        entered((w, 0))
    pre(0, 0, 8)
    gather_step(second, 3)
    for k0, n in ((0, 4), (4, 4)):
        post_rows(0, k0, n)
    gather_step(second, 4)
    entered(("wg", 1))
    entered(("wu", 1))
    pre(1, 0, 8)
    entered(("wd", 1))
    batches = ((7, 1, (4,)), (5, 2, (3, 5)), (3, 2, (2, 6)), (0, 3, (0, 1, 7)))
    for k0, n, ds in batches:
        post_rows(1, k0, n)
        for d in ds:
            put(0, PLACE[d])
            give_mate(0, d)
        if k0 == 5:
            scatter_far(0)
    scatter_open(0)
    for d in range(RING):
        gathered("x1", d)
    each(lambda k: pick(1, x1, xg, k))
    each(lambda k: pick_scales(1, k))
    scatter_step(0, 3)
    pre(0, 0, 8)
    scatter_step(0, 2)
    pre(1, 0, 8)
    scatter_step(0, 1)
    sent[0, "rc", 0].wait_recv()
    for ch in range(2):
        tot[0, rows(ch)] = scatter_last(0, ch, g0)
        send(("pass", ch), tot.at[0, rows(ch)], g1.at[0, 0, rows(ch)], pass_to)

    for ch in range(2):
        sent["pass", ch].wait_recv()
        gather_first("g1", g1, ch)
    third = (("g1", g1),)
    for d in (1, 2, 3, 4):
        gather_step(third, d)
        if d == 1:
            ds = (0,)
        elif d == 2:
            ds = (1, 7)
        elif d == 3:
            ds = (2, 6)
        else:
            ds = (3, 5)
        for q in ds:
            gathered("g1", q)
            pick(1, g1, gg, PLACE[q])
        if d > 1:
            k0, n = {2: (0, 3), 3: (3, 2), 4: (5, 2)}[d]
            for j in range(2):
                post_rows(j, k0, n)
            for q in (0, 1, 7) if d == 2 else ds:
                put(1, PLACE[q])
                give_mate(1, q)
    gathered("g1", 4)
    pick(1, g1, gg, 7)
    for j in range(2):
        post_rows(j, 7, 1)
    put(1, 7)
    give_mate(1, 4)
    scatter_open(1)
    scatter_far(1)
    scatter_step(1, 3)
    scatter_step(1, 2)
    scatter_step(1, 1)
    sent[1, "rc", 0].wait_recv()
    finals = []
    for ch in range(2):
        tot[1, rows(ch)] = scatter_last(1, ch, g1)
        enter(("fin", ch), tot.at[1, rows(ch)], fin.at[rows(ch)])
    for ch in range(2):
        entered(("fin", ch))
    out_ref[...] = fin[...]

    for copy in sent.values():
        copy.wait_send()

    @pl.when(mixed)
    def _():
        for _, copy in moves.values():
            copy.wait_send()


def shards(grad_out, saved_inputs, routes, gate_weights, w_gate, w_up, w_down):
    table = jnp.concatenate(
        [
            jnp.swapaxes(routes[0], 1, 2).astype(F32),
            jnp.swapaxes(gate_weights[0], 1, 2),
        ],
        axis=1,
    )
    block = pltpu.VMEM((RING, 2, TOK, D), BF)
    return pl.pallas_call(
        kernel,
        out_shape=jax.ShapeDtypeStruct((TOK, D), BF),
        in_specs=[pl.BlockSpec(memory_space=pl.ANY)] * 6,
        out_specs=pl.BlockSpec(memory_space=pltpu.VMEM),
        scratch_shapes=[
            block, block, block, block,
            pltpu.VMEM((RING, 2, 2, 16, TOK), F32),
            pltpu.VMEM((2, D, H), BF),
            pltpu.VMEM((2, D, H), BF),
            pltpu.VMEM((2, H, D), BF),
            pltpu.VMEM((2, RING, 2, TOK, D), BF),
            pltpu.VMEM((2, RING, TOK, D), BF),
            pltpu.VMEM((2, 4, TOK, D), BF),
            pltpu.VMEM((2, 4, TOK, D), BF),
            pltpu.VMEM((2, TOK, D), BF),
            pltpu.VMEM((TOK, D), BF),
            pltpu.VMEM((2, RING * CAP, D), BF),
            pltpu.VMEM((2, RING * CAP, D), BF),
            pltpu.VMEM((2, RING * CAP, H), F32),
            pltpu.VMEM((2, RING * CAP, H), F32),
            pltpu.VMEM((RING, 2 * CAP, D), BF),
            pltpu.VMEM((2, RING * CAP, 1), F32),
            pltpu.VMEM((2, 16, 256), F32),
            pltpu.VMEM((2, RING, 256, 2), F32),
            pltpu.SemaphoreType.DMA((SEMS,)),
            pltpu.SemaphoreType.DMA((SEMS,)),
            pltpu.SemaphoreType.DMA((16,)),
        ],
        compiler_params=pltpu.CompilerParams(
            collective_id=0, has_side_effects=True, vmem_limit_bytes=63 << 20
        ),
        name="moe_back",
    )(grad_out[0], saved_inputs[0], table, w_gate[0], w_up[0], w_down[0])[None]


def solution(mesh):
    placed = (
        P("section", "expert", None),
        P("section", None, "expert", None),
        P("section", None, "expert", None),
        P("section", None, "expert", None),
        P("section", "expert", None, None),
        P("section", "expert", None, None),
        P("section", "expert", None, None),
    )
    return jax.shard_map(
        shards, mesh=mesh, in_specs=placed, out_specs=P("section", "expert", None), check_vma=False
    )
```

```python
import jax
import jax.numpy as jnp
from jax import lax
from jax.experimental import pallas as pl
from jax.experimental.pallas import tpu as pltpu
from jax.sharding import PartitionSpec as P

BF = jnp.bfloat16
F32 = jnp.float32
TOK = 128
D = 1024
H = 512
CAP = 80
RING = 8
PLACE = {0: 0, 1: 1, 7: 2, 2: 3, 6: 4, 3: 5, 5: 6, 4: 7}
SENDERS = 40
TAKERS = 190


def nt(a, b):
    return lax.dot_general(a, b, (((1,), (1,)), ((), ())), preferred_element_type=F32)


def nn(a, b):
    return lax.dot_general(a, b, (((1,), (0,)), ((), ())), preferred_element_type=F32)


def kernel(
    grad_in, saved_in, routes_in, weights_in, wg_in, wu_in, wd_in, out_ref,
    xg0, x1, g1, tab, wg, wu, wd, part, l_core, l_down, l_up, tot, fin,
    xg, gg, gp, up, rw, ws, pos, post, own_routes, own_table, ssem, rsem, lsem,
):
    s = lax.axis_index("section")
    e = lax.axis_index("expert")
    core = lax.rem(s, 2)
    x_lo = lax.rem(e, 2)
    mixed = core != x_lo
    other_core = s + 1 - 2 * core
    other_x = e + 1 - 2 * x_lo
    z_up = (s, lax.rem(e + 2, 16))
    z_down = (s, lax.rem(e + 14, 16))
    mate = (other_core, e)
    swap = (other_core, other_x)
    pass_to = (lax.rem(s + 16 - 2 * (1 - x_lo), 16), other_x)
    pass_from = (lax.rem(s + 2 * x_lo, 16), other_x)
    home = lax.select(mixed, other_x, e)

    barrier = pltpu.get_barrier_semaphore()
    for peer in (z_up, z_down, mate, swap, pass_to, pass_from):
        pl.semaphore_signal(barrier, inc=1, device_id=peer, device_id_type=pl.DeviceIdType.MESH)

    senders, takers, sent, ends = {}, {}, {}, []

    def number(table, key):
        return table.setdefault(key, len(table))

    def make(batch, group, src, dst, peer):
        return pltpu.make_async_remote_copy(
            src_ref=src, dst_ref=dst,
            send_sem=ssem.at[number(senders, batch)], recv_sem=rsem.at[number(takers, group)],
            device_id=peer, device_id_type=pl.DeviceIdType.MESH,
        )

    def send(key, src, dst, peer, batch):
        sent[key] = make(batch, key, src, dst, peer)
        sent[key].start()

    moves = {}

    def enter(key, pairs, whole):
        i = number(moves, key)

        @pl.when(jnp.logical_not(mixed))
        def _():
            for src, dst in pairs:
                pltpu.make_async_copy(src, dst, lsem.at[i]).start()

        @pl.when(mixed)
        def _():
            for src, dst in pairs:
                make(key, key, src, dst, swap).start()

        ends.append((key, whole))

    def entered(key):
        whole = dict(ends)[key]

        @pl.when(jnp.logical_not(mixed))
        def _():
            pltpu.make_async_copy(whole, whole, lsem.at[moves[key]]).wait()

        @pl.when(mixed)
        def _():
            make(key, key, whole, whole, swap).wait_recv()

    loads = [
        pltpu.make_async_copy(routes_in, own_routes, lsem.at[18]),
        pltpu.make_async_copy(weights_in, own_table.at[:, 8:16], lsem.at[19]),
    ]
    for load in loads:
        load.start()
    pl.semaphore_wait(barrier, 6)
    for ch in range(2):
        at = pl.ds(64 * ch, 64)
        enter(
            ("a", ch),
            [
                (saved_in.at[0, at], xg0.at[0, 0, 0, at]),
                (grad_in.at[at], xg0.at[0, 0, 1, at]),
            ],
            xg0.at[0, 0, :, at],
        )
    for load in loads:
        load.wait()
    own_table[:, 0:8] = own_routes[...].astype(F32)
    enter("t", [(own_table, tab.at[0, 0])], tab.at[0, 0])
    for j in range(2):
        for name, src, dst in (("wg", wg_in, wg), ("wu", wu_in, wu), ("wd", wd_in, wd)):
            enter((name, j), [(src.at[j], dst.at[j])], dst.at[j])
        if j == 0:
            enter("x1", [(saved_in.at[1], x1.at[0, 0])], x1.at[0, 0])

    def rows(ch, n):
        return pl.ds(TOK // n * ch, TOK // n)

    def upper(ch, n):
        return ch < n // 2

    def piece(buf, k, c, at):
        return buf.at[k, c, :, at] if len(buf.shape) == 5 else buf.at[k, c, at]

    def to_mate(name, buf, d, ch, n):
        k = PLACE[d]
        at = rows(ch, n)
        make((name, "c"), (name, "c", d), piece(buf, k, 0, at), piece(buf, k, 1, at), mate).start()

    def gathered(name, buf, d):
        k = PLACE[d]
        make((name, "c"), (name, "c", d), buf.at[k, 0], buf.at[k, 1], mate).wait_recv()

    def hop(name, buf, way, d, ch, n):
        src, dst = (d, d + 1) if way == "u" else ((8 - d) % 8, 7 - d)
        at = rows(ch, n)
        send(
            (name, way, d, ch),
            piece(buf, PLACE[src], 0, at),
            piece(buf, PLACE[dst], 0, at),
            z_up if way == "u" else z_down,
            (name, "z"),
        )

    def gather_first(name, buf, ch, n):
        hop(name, buf, "u", 0, ch, n)
        hop(name, buf, "d", 0, ch, n)
        to_mate(name, buf, 0, ch, n)

    def gather_step(name, buf, d, chs, n):
        for ch in chs:
            for way in "ud":
                here = d if way == "u" else 8 - d
                half = (way == "u") == upper(ch, n)
                if d < 4 or half:
                    sent[name, way, d - 1, ch].wait_recv()
                    if d < 3 or (d == 3 and half):
                        hop(name, buf, way, d, ch, n)
                    to_mate(name, buf, here, ch, n)

    def table_step(d):
        def on(way, d, k, to, peer):
            send(("t", way, d), tab.at[k, 0], tab.at[to, 0], peer, ("t", "z"))

        def across(d, k):
            make(("t", "c"), ("t", "c"), tab.at[k, 0], tab.at[k, 1], mate).start()

        if d == 0:
            on("u", 0, 0, PLACE[1], z_up)
            on("d", 0, 0, PLACE[7], z_down)
            across(0, 0)
            return
        sent["t", "u", d - 1].wait_recv()
        k = PLACE[d]
        if d < 4:
            on("u", d, k, PLACE[d + 1], z_up)
        across(d, k)
        if d < 4:
            sent["t", "d", d - 1].wait_recv()
            k = PLACE[8 - d]
            if d < 3:
                on("d", d, k, PLACE[7 - d], z_down)
            across(8 - d, k)

    def tables_there():
        make(("t", "c"), ("t", "c"), tab.at[:, 0], tab.at[:, 1], mate).wait_recv()

    def places(t):
        masks = []
        for k in range(RING):
            named = jnp.concatenate([tab[k, 0, t, 0:8], tab[k, 1, t, 0:8]], axis=1)
            for j in range(2):
                hit = named == (2 * home + j).astype(F32)
                masks.append(jnp.sum(jnp.where(hit, 1.0, 0.0), axis=0, keepdims=True))
        mask = jnp.concatenate(masks, axis=0)
        before = lax.broadcasted_iota(jnp.int32, (256, 256), 0) < lax.broadcasted_iota(
            jnp.int32, (256, 256), 1
        )
        earlier = nn(mask.astype(BF), jnp.where(before, 1.0, 0.0).astype(BF))
        where = jnp.where(mask > 0.5, earlier, -1000.0)
        pos[t] = where
        turned = jnp.transpose(jnp.concatenate([where, jnp.zeros((112, 256), F32)], axis=0))
        for k in range(RING):
            post[t, k] = turned[:, 2 * k : 2 * k + 2]

    def chosen(t, k):
        slot = lax.broadcasted_iota(jnp.int32, (CAP, 256), 0).astype(F32)
        return [slot == pos[t, pl.ds(2 * k + j, 1)] for j in range(2)]

    def pick(t, src, dst, k):
        hot = jnp.concatenate([jnp.where(h, 1.0, 0.0) for h in chosen(t, k)], axis=0).astype(BF)
        got = nn(hot, src.reshape(256, D)).astype(BF)
        at = pl.ds(pl.multiple_of(k * CAP, 16), CAP)
        dst[0, at] = got[:CAP]
        dst[1, at] = got[CAP:]

    def pick_scales(t, k):
        named = jnp.concatenate([tab[k, 0, t, 0:8], tab[k, 1, t, 0:8]], axis=1)
        weight = jnp.concatenate([tab[k, 0, t, 8:16], tab[k, 1, t, 8:16]], axis=1)
        at = pl.ds(pl.multiple_of(k * CAP, 16), CAP)
        for j, h in enumerate(chosen(t, k)):
            mine = jnp.sum(
                jnp.where(named == (2 * home + j).astype(F32), weight, 0.0), axis=0, keepdims=True
            )
            ws[j, at] = jnp.sum(jnp.where(h, mine, 0.0), axis=1, keepdims=True)

    def pre(j, k0, n):
        at = pl.ds(k0 * CAP, n * CAP)
        x = xg[j, at]
        gp[j, at] = nn(x, wg[j])
        up[j, at] = nn(x, wu[j])

    def post_rows(j, k0, n):
        at = pl.ds(k0 * CAP, n * CAP)
        hidden = nt(gg[j, at], wd[j])
        gate = gp[j, at]
        sig = 1.0 / (1.0 + jnp.exp(-gate))
        hs = hidden * sig
        gate_grad = (hs * up[j, at] * (1.0 + gate * (1.0 - sig))).astype(BF)
        up_grad = (hs * gate).astype(BF)
        grown = nt(gate_grad, wg[j]) + nt(up_grad, wu[j])
        grown = (grown * ws[j, at]).astype(BF)
        for i in range(n):
            rw[k0 + i, j * CAP : (j + 1) * CAP] = grown[i * CAP : (i + 1) * CAP]

    def put(t, k):
        lane = lax.broadcasted_iota(jnp.int32, (256, 2 * CAP), 1).astype(F32)
        col = post[t, k]
        hot = jnp.logical_or(lane == col[:, 0:1], lane == col[:, 1:2] + float(CAP))
        summed = nn(jnp.where(hot, 1.0, 0.0).astype(BF), rw[k])
        part[t, k] = summed.astype(BF).reshape(2, TOK, D)

    def give_mate(t, d):
        k = PLACE[d]
        send((t, "rc", d), part.at[t, k, 1], l_core.at[t, k], mate, (t, "rc"))

    def give(t, way, d, ch):
        src = part.at[t, PLACE[d], 0, rows(ch, 4)]
        if way == "d":
            send((t, "rd", d, ch), src, l_down.at[t, d - 1, rows(ch, 4)], z_down, (t, "rz"))
        else:
            send((t, "ru", d, ch), src, l_up.at[t, 7 - d, rows(ch, 4)], z_up, (t, "rz"))

    def add_up(t, way, d, ch, arrived):
        k = PLACE[d]
        at = rows(ch, 4)
        value = part[t, k, 0, at].astype(F32) + l_core[t, k, at].astype(F32)
        if arrived:
            landed = l_down[t, d, at] if way == "d" else l_up[t, 8 - d, at]
            value = value + landed.astype(F32)
        part[t, k, 0, at] = value.astype(BF)

    def scatter_open(t):
        sent[t, "rc", 3].wait_recv()
        sent[t, "rc", 5].wait_recv()
        for i in range(2):
            for way, d, ch in (("d", 3, 2 + i), ("u", 5, i)):
                add_up(t, way, d, ch, False)
                give(t, way, d, ch)

    def scatter_far(t):
        sent[t, "rc", 4].wait_recv()
        for i in range(2):
            for way, ch in (("d", i), ("u", 2 + i)):
                add_up(t, way, 4, ch, False)
                give(t, way, 4, ch)

    def scatter_step(t, n):
        turns = {3: ((0, 2), (1, 3)), 2: ((2, 0), (0, 2), (3, 1), (1, 3)), 1: ((0, 0), (2, 2), (1, 1), (3, 3))}[n]
        if n != 3:
            sent[t, "rc", n].wait_recv()
            sent[t, "rc", 8 - n].wait_recv()
        for ch_d, ch_u in turns:
            for way, d, ch in (("d", n, ch_d), ("u", 8 - n, ch_u)):
                back = d + 1 if way == "d" else d - 1
                sent[t, "r" + way, back, ch].wait_recv()
                add_up(t, way, d, ch, True)
                give(t, way, d, ch)

    def scatter_last(t, ch, own):
        sent[t, "rd", 1, ch].wait_recv()
        sent[t, "ru", 7, ch].wait_recv()
        at = rows(ch, 4)
        tot[t, at] = (
            own[at].astype(F32)
            + (part[t, 0, 0, at].astype(F32) + l_core[t, 0, at].astype(F32))
            + (l_down[t, 0, at].astype(F32) + l_up[t, 0, at].astype(F32))
        ).astype(BF)

    def each(body):
        def step(k, carry):
            body(k)
            return carry

        lax.fori_loop(0, RING, step, 0)

    for ch in range(2):
        entered(("a", ch))
        gather_first("a", xg0, ch, 2)
    entered("t")
    table_step(0)
    for d in (1, 2, 3, 4):
        gather_step("a", xg0, d, (0, 1), 2)
        table_step(d)
        if d == 3:
            entered("x1")
            for ch in range(2):
                gather_first("x1", x1, ch, 2)
    tables_there()
    places(0)
    places(1)
    for d in range(RING):
        gathered("a", xg0, d)
    gather_step("x1", x1, 1, (0, 1), 2)

    def pick0(k):
        pick(0, xg0[k, :, 0], xg, k)
        pick(0, xg0[k, :, 1], gg, k)
        pick_scales(0, k)

    each(pick0)
    gather_step("x1", x1, 2, (0, 1), 2)
    for w in ("wg", "wu", "wd"):
        entered((w, 0))
    pre(0, 0, 8)
    gather_step("x1", x1, 3, (0, 1), 2)
    for k0, n in ((0, 4), (4, 4)):
        post_rows(0, k0, n)
    gather_step("x1", x1, 4, (0, 1), 2)
    for d in range(RING):
        gathered("x1", x1, d)
    entered(("wg", 1))
    entered(("wu", 1))
    pre(1, 0, 8)
    each(lambda k: pick(1, x1[k], xg, k))
    entered(("wd", 1))

    def finish(t, ds):
        for d in ds:
            put(t, PLACE[d])
            give_mate(t, d)

    post_rows(1, 5, 3)
    finish(0, (3, 5, 4))
    post_rows(1, 3, 2)
    scatter_open(0)
    scatter_far(0)
    finish(0, (2, 6))
    post_rows(1, 0, 3)
    finish(0, (1, 7, 0))
    scatter_step(0, 3)
    pre(0, 0, 8)
    scatter_step(0, 2)
    pre(1, 0, 8)
    each(lambda k: pick_scales(1, k))
    scatter_step(0, 1)
    sent[0, "rc", 0].wait_recv()
    order = (0, 2, 1, 3)

    def passing(ch):
        scatter_last(0, ch, xg0.at[0, 0, 1])
        at = rows(ch, 4)
        send(("pass", ch), tot.at[0, at], g1.at[0, 0, at], pass_to, "pass")

    def passed(ch):
        sent["pass", ch].wait_recv()
        gather_first("g1", g1, ch, 4)

    passing(0)
    passing(2)
    passed(0)
    passing(1)
    passed(2)
    passing(3)
    passed(1)
    passed(3)

    def level(d, ch):
        gather_step("g1", g1, d, (ch,), 4)

    def take(ds):
        for d in ds:
            gathered("g1", g1, d)
            pick(1, g1[PLACE[d]], gg, PLACE[d])

    for ch in order:
        level(1, ch)
    take((0,))
    level(2, 0)
    level(2, 2)
    take((1, 7))
    level(2, 1)
    post_rows(0, 0, 3)
    level(2, 3)
    post_rows(1, 0, 3)
    level(3, 0)
    finish(1, (1, 7, 0))
    level(3, 2)
    take((2, 6))
    post_rows(0, 3, 2)
    level(3, 1)
    post_rows(1, 3, 2)
    level(3, 3)
    finish(1, (2, 6))
    level(4, 0)
    level(4, 2)
    take((3, 5))
    post_rows(0, 5, 2)
    level(4, 1)
    level(4, 3)
    post_rows(1, 5, 2)
    finish(1, (3, 5))
    take((4,))
    post_rows(0, 7, 1)
    scatter_open(1)
    post_rows(1, 7, 1)
    finish(1, (4,))
    scatter_far(1)
    scatter_step(1, 3)
    scatter_step(1, 2)
    scatter_step(1, 1)
    sent[1, "rc", 0].wait_recv()
    for ch in order:
        scatter_last(1, ch, g1.at[0, 0])
        enter(("fin", ch), [(tot.at[1, rows(ch, 4)], fin.at[rows(ch, 4)])], fin.at[rows(ch, 4)])
    for ch in order:
        entered(("fin", ch))
        out_ref[rows(ch, 4)] = fin[rows(ch, 4)]

    for name, buf in (("a", xg0), ("x1", x1), ("g1", g1), ("t", tab)):
        group = ("t", "c") if name == "t" else (name, "c", 0)
        make((name, "z"), group, buf.at[0:7, 0], buf.at[0:7, 1], z_up).wait_send()
        make((name, "c"), group, buf.at[:, 0], buf.at[:, 1], mate).wait_send()
    for t in range(2):
        make((t, "rz"), (t, "rc", 0), part.at[t, 0:7, 0], part.at[t, 0:7, 0], z_up).wait_send()
        make((t, "rc"), (t, "rc", 0), part.at[t, :, 1], part.at[t, :, 1], mate).wait_send()
    make("pass", ("pass", 0), tot.at[0], tot.at[0], pass_to).wait_send()

    @pl.when(mixed)
    def _():
        for key, whole in ends:
            make(key, key, whole, whole, swap).wait_send()

    assert len(senders) <= SENDERS and len(takers) <= TAKERS, (len(senders), len(takers))

def shards(grad_out, saved_inputs, routes, gate_weights, w_gate, w_up, w_down):
    block = pltpu.VMEM((RING, 2, TOK, D), BF)
    return pl.pallas_call(
        kernel,
        out_shape=jax.ShapeDtypeStruct((TOK, D), BF),
        in_specs=[pl.BlockSpec(memory_space=pl.ANY)] * 7,
        out_specs=pl.BlockSpec(memory_space=pltpu.VMEM),
        scratch_shapes=[
            pltpu.VMEM((RING, 2, 2, TOK, D), BF),
            block, block,
            pltpu.VMEM((RING, 2, 2, 16, TOK), F32),
            pltpu.VMEM((2, D, H), BF),
            pltpu.VMEM((2, D, H), BF),
            pltpu.VMEM((2, H, D), BF),
            pltpu.VMEM((2, RING, 2, TOK, D), BF),
            pltpu.VMEM((2, RING, TOK, D), BF),
            pltpu.VMEM((2, 4, TOK, D), BF),
            pltpu.VMEM((2, 4, TOK, D), BF),
            pltpu.VMEM((2, TOK, D), BF),
            pltpu.VMEM((TOK, D), BF),
            pltpu.VMEM((2, RING * CAP, D), BF),
            pltpu.VMEM((2, RING * CAP, D), BF),
            pltpu.VMEM((2, RING * CAP, H), F32),
            pltpu.VMEM((2, RING * CAP, H), F32),
            pltpu.VMEM((RING, 2 * CAP, D), BF),
            pltpu.VMEM((2, RING * CAP, 1), F32),
            pltpu.VMEM((2, 16, 256), F32),
            pltpu.VMEM((2, RING, 256, 2), F32),
            pltpu.VMEM((2, 8, TOK), jnp.int32),
            pltpu.VMEM((2, 16, TOK), F32),
            pltpu.SemaphoreType.DMA((SENDERS,)),
            pltpu.SemaphoreType.DMA((TAKERS,)),
            pltpu.SemaphoreType.DMA((20,)),
        ],
        compiler_params=pltpu.CompilerParams(
            collective_id=0, has_side_effects=True, vmem_limit_bytes=63 << 20
        ),
        name="moe_back",
    )(
        grad_out[0],
        saved_inputs[0],
        jnp.swapaxes(routes[0], 1, 2),
        jnp.swapaxes(gate_weights[0], 1, 2),
        w_gate[0],
        w_up[0],
        w_down[0],
    )[None]


def solution(mesh):
    placed = (
        P("section", "expert", None),
        P("section", None, "expert", None),
        P("section", None, "expert", None),
        P("section", None, "expert", None),
        P("section", "expert", None, None),
        P("section", "expert", None, None),
        P("section", "expert", None, None),
    )
    return jax.shard_map(
        shards, mesh=mesh, in_specs=placed, out_specs=P("section", "expert", None), check_vma=False
    )
```

```python
import jax
import jax.numpy as jnp
from jax import lax
from jax.experimental import pallas as pl
from jax.experimental.pallas import tpu as pltpu
from jax.sharding import PartitionSpec as P

BF = jnp.bfloat16
F32 = jnp.float32
TOK = 128
D = 1024
H = 512
CAP = 80
RING = 8
PLACE = {0: 0, 1: 1, 7: 2, 2: 3, 6: 4, 3: 5, 5: 6, 4: 7}
SENDERS = 40
TAKERS = 162
FINE = 8


def nt(a, b):
    return lax.dot_general(a, b, (((1,), (1,)), ((), ())), preferred_element_type=F32)


def nn(a, b):
    return lax.dot_general(a, b, (((1,), (0,)), ((), ())), preferred_element_type=F32)


def kernel(
    grad_in, saved_in, routes_in, weights_in, wg_in, wu_in, wd_in, out_ref,
    xg0, x1, g1, tab, wg, wu, wd, part, l_core, l_down, l_up, tot,
    xg, gg, gp, up, rw, ws, pos_full, post_full, pos_half, post_half, own_routes, own_table, ssem, rsem, lsem,
):
    s = lax.axis_index("section")
    e = lax.axis_index("expert")
    core = lax.rem(s, 2)
    x_lo = lax.rem(e, 2)
    mixed = core != x_lo
    other_core = s + 1 - 2 * core
    other_x = e + 1 - 2 * x_lo
    z_up = (s, lax.rem(e + 2, 16))
    z_down = (s, lax.rem(e + 14, 16))
    mate = (other_core, e)
    swap = (other_core, other_x)
    pass_to = (lax.rem(s + 16 - 2 * (1 - x_lo), 16), other_x)
    pass_from = (lax.rem(s + 2 * x_lo, 16), other_x)
    home = lax.select(mixed, other_x, e)

    barrier = pltpu.get_barrier_semaphore()
    for peer in (z_up, z_down, mate, swap, pass_to, pass_from):
        pl.semaphore_signal(barrier, inc=1, device_id=peer, device_id_type=pl.DeviceIdType.MESH)

    senders, takers, sent, ends = {}, {}, {}, []

    def number(table, key):
        return table.setdefault(key, len(table))

    def make(batch, group, src, dst, peer):
        if group[0] == 1:
            group = (0,) + group[1:]
        elif group[0] == "g1" and group[1] == "c":
            group = ("a",) + group[1:]
        elif group[0] == "g1":
            place = 4 if group[2] == 3 else 3 - group[2]
            group = (0, "r" + group[1], place if group[1] == "d" else 8 - place, group[3])
        return pltpu.make_async_remote_copy(
            src_ref=src, dst_ref=dst,
            send_sem=ssem.at[number(senders, batch)], recv_sem=rsem.at[number(takers, group)],
            device_id=peer, device_id_type=pl.DeviceIdType.MESH,
        )

    def send(key, src, dst, peer, batch):
        sent[key] = make(batch, key, src, dst, peer)
        sent[key].start()

    moves = {}

    def enter(key, pairs, whole):
        i = number(moves, key)

        @pl.when(jnp.logical_not(mixed))
        def _():
            for src, dst in pairs:
                pltpu.make_async_copy(src, dst, lsem.at[i]).start()

        @pl.when(mixed)
        def _():
            for src, dst in pairs:
                make(key, key, src, dst, swap).start()

        ends.append((key, whole))

    def entered(key):
        whole = dict(ends)[key]

        @pl.when(jnp.logical_not(mixed))
        def _():
            pltpu.make_async_copy(whole, whole, lsem.at[moves[key]]).wait()

        @pl.when(mixed)
        def _():
            make(key, key, whole, whole, swap).wait_recv()

    loads = [
        pltpu.make_async_copy(routes_in, own_routes, lsem.at[18]),
        pltpu.make_async_copy(weights_in, own_table.at[:, 8:16], lsem.at[19]),
    ]
    for load in loads:
        load.start()
    pl.semaphore_wait(barrier, 6)
    for ch in range(2):
        at = pl.ds(64 * ch, 64)
        enter(
            ("a", ch),
            [
                (saved_in.at[0, at], xg0.at[0, 0, 0, at]),
                (grad_in.at[at], xg0.at[0, 0, 1, at]),
            ],
            xg0.at[0, 0, :, at],
        )
    for load in loads:
        load.wait()
    own_table[:, 0:8] = own_routes[...].astype(F32)
    enter("t", [(own_table, tab.at[0, 0])], tab.at[0, 0])
    for j in range(2):
        for name, src, dst in (("wg", wg_in, wg), ("wu", wu_in, wu), ("wd", wd_in, wd)):
            enter((name, j), [(src.at[j], dst.at[j])], dst.at[j])
        if j == 0:
            enter("x1", [(saved_in.at[1], x1.at[0, 0])], x1.at[0, 0])

    def rows(ch, n):
        return pl.ds(TOK // n * ch, TOK // n)

    def upper(ch, n):
        return ch % 2 == 0 if n == 2 else ch // 2 % 2 == 0

    def piece(buf, k, c, at):
        return buf.at[k, c, :, at] if len(buf.shape) == 5 else buf.at[k, c, at]

    def to_mate(name, buf, d, ch, n):
        k = PLACE[d]
        at = rows(ch, n)
        group = (name, "c", d, 2 * ch // n if n == FINE else 0)
        make((name, "c"), group, piece(buf, k, 0, at), piece(buf, k, 1, at), mate).start()

    def gathered(name, buf, d, h=0, at=pl.ds(0, TOK)):
        k = PLACE[d]
        group = (name, "c", d, h)
        make((name, "c"), group, piece(buf, k, 0, at), piece(buf, k, 1, at), mate).wait_recv()

    def hop(name, buf, way, d, ch, n):
        src, dst = (d, d + 1) if way == "u" else ((8 - d) % 8, 7 - d)
        at = rows(ch, n)
        send(
            (name, way, d, ch),
            piece(buf, PLACE[src], 0, at),
            piece(buf, PLACE[dst], 0, at),
            z_up if way == "u" else z_down,
            (name, "z"),
        )

    def gather_first(name, buf, ch, n):
        hop(name, buf, "u", 0, ch, n)
        hop(name, buf, "d", 0, ch, n)
        to_mate(name, buf, 0, ch, n)

    def gather_step(name, buf, d, chs, n):
        for pair in chs:
            for way, ch in zip("ud", pair):
                here = d if way == "u" else 8 - d
                half = (way == "u") == upper(ch, n)
                if d < 4 or half:
                    sent[name, way, d - 1, ch].wait_recv()
                    if d < 3 or (d == 3 and half):
                        hop(name, buf, way, d, ch, n)
                    to_mate(name, buf, here, ch, n)

    def table_step(d):
        def on(way, d, k, to, peer):
            send(("t", way, d), tab.at[k, 0], tab.at[to, 0], peer, ("t", "z"))

        def across(d, k):
            make(("t", "c"), ("t", "c"), tab.at[k, 0], tab.at[k, 1], mate).start()

        if d == 0:
            on("u", 0, 0, PLACE[1], z_up)
            on("d", 0, 0, PLACE[7], z_down)
            across(0, 0)
            return
        sent["t", "u", d - 1].wait_recv()
        k = PLACE[d]
        if d < 4:
            on("u", d, k, PLACE[d + 1], z_up)
        across(d, k)
        if d < 4:
            sent["t", "d", d - 1].wait_recv()
            k = PLACE[8 - d]
            if d < 3:
                on("d", d, k, PLACE[7 - d], z_down)
            across(8 - d, k)

    def tables_there():
        make(("t", "c"), ("t", "c"), tab.at[:, 0], tab.at[:, 1], mate).wait_recv()

    def half(h):
        return pl.ds(0, TOK) if h is None else pl.ds(64 * h, 64)

    def lanes(k, t, h, first):
        both = [tab[k, c, t, first : first + 8] for c in range(2)]
        if h is not None:
            both = [v[:, 64 * h : 64 * h + 64] for v in both]
        return jnp.concatenate(both, axis=1)

    def places(t, h, pos, post):
        masks = []
        for k in range(RING):
            named = lanes(k, t, h, 0)
            for j in range(2):
                hit = named == (2 * home + j).astype(F32)
                masks.append(jnp.sum(jnp.where(hit, 1.0, 0.0), axis=0, keepdims=True))
        mask = jnp.concatenate(masks, axis=0)
        n = mask.shape[1]
        before = lax.broadcasted_iota(jnp.int32, (n, n), 0) < lax.broadcasted_iota(
            jnp.int32, (n, n), 1
        )
        earlier = nn(mask.astype(BF), jnp.where(before, 1.0, 0.0).astype(BF))
        where = jnp.where(mask > 0.5, earlier, -1000.0)
        pos[...] = where
        turned = jnp.transpose(jnp.concatenate([where, jnp.zeros((112, n), F32)], axis=0))
        for k in range(RING):
            post[k] = turned[:, 2 * k : 2 * k + 2]

    def chosen(pos, k):
        slot = lax.broadcasted_iota(jnp.int32, (CAP, pos.shape[1]), 0).astype(F32)
        return [slot == pos[pl.ds(2 * k + j, 1)] for j in range(2)]

    def unit_rows(k):
        return pl.ds(pl.multiple_of(k * CAP, 16), CAP)

    def pos_of(h):
        return pos_full if h is None else pos_half.at[h]

    def pick(h, tokens, dst, k):
        pos = pos_of(h)
        hot = jnp.concatenate([jnp.where(c, 1.0, 0.0) for c in chosen(pos, k)], axis=0).astype(BF)
        got = nn(hot, tokens.reshape(pos.shape[1], D)).astype(BF)
        dst[0, unit_rows(k)] = got[:CAP]
        dst[1, unit_rows(k)] = got[CAP:]

    def pick_scales(t, h, k):
        named = lanes(k, t, h, 0)
        weight = lanes(k, t, h, 8)
        for j, hit in enumerate(chosen(pos_of(h), k)):
            mine = jnp.sum(
                jnp.where(named == (2 * home + j).astype(F32), weight, 0.0), axis=0, keepdims=True
            )
            ws[t + (h or 0), j, unit_rows(k)] = jnp.sum(jnp.where(hit, mine, 0.0), axis=1, keepdims=True)

    def pre(h, j):
        x = xg[j]
        gp[h, j] = nn(x, wg[j])
        up[h, j] = nn(x, wu[j])

    def post_rows(t, h, j, k0, n):
        at = pl.ds(k0 * CAP, n * CAP)
        hidden = nt(gg[j, at], wd[j])
        gate = gp[h, j, at]
        sig = 1.0 / (1.0 + jnp.exp(-gate))
        hs = hidden * sig
        gate_grad = (hs * up[h, j, at] * (1.0 + gate * (1.0 - sig))).astype(BF)
        up_grad = (hs * gate).astype(BF)
        grown = nt(gate_grad, wg[j]) + nt(up_grad, wu[j])
        grown = (grown * ws[t + h, j, at]).astype(BF)
        for i in range(n):
            rw[k0 + i, j * CAP : (j + 1) * CAP] = grown[i * CAP : (i + 1) * CAP]

    def put(t, h, k):
        col = post_full[k] if h is None else post_half[h, k]
        lane = lax.broadcasted_iota(jnp.int32, (col.shape[0], 2 * CAP), 1).astype(F32)
        hot = jnp.logical_or(lane == col[:, 0:1], lane == col[:, 1:2] + float(CAP))
        summed = nn(jnp.where(hot, 1.0, 0.0).astype(BF), rw[k]).astype(BF)
        part[t, k, :, half(h)] = summed.reshape(2, col.shape[0] // 2, D)

    def halved(t, h, d):
        return h if t == 1 else None

    def give_mate(t, h, d):
        k = PLACE[d]
        h = halved(t, h, d)
        at = half(h)
        send((t, "rc", d, h or 0), part.at[t, k, 1, at], l_core.at[t, k, at], mate, (t, "rc"))

    there = set()

    def mate_there(t, h, *ds):
        for d in ds:
            key = (t, "rc", d, halved(t, h, d) or 0)
            if key not in there:
                there.add(key)
                sent[key].wait_recv()

    def give(t, way, d, ch):
        src = part.at[t, PLACE[d], 0, rows(ch, FINE)]
        if way == "d":
            send((t, "rd", d, ch), src, l_down.at[t, d - 1, rows(ch, FINE)], z_down, (t, "rz"))
        else:
            send((t, "ru", d, ch), src, l_up.at[t, 7 - d, rows(ch, FINE)], z_up, (t, "rz"))

    def add_up(t, way, d, ch, arrived):
        k = PLACE[d]
        at = rows(ch, FINE)
        value = part[t, k, 0, at].astype(F32) + l_core[t, k, at].astype(F32)
        if arrived:
            landed = l_down[t, d, at] if way == "d" else l_up[t, 8 - d, at]
            value = value + landed.astype(F32)
        part[t, k, 0, at] = value.astype(BF)

    def far(t, h):
        mate_there(t, h, 4)
        for i in range(2):
            for way, ch in (("d", 4 * h + i), ("u", 4 * h + 2 + i)):
                add_up(t, way, 4, ch, False)
                give(t, way, 4, ch)

    def near(t, h):
        mate_there(t, h, 3, 5)
        for i in range(2):
            for way, d, ch in (("d", 3, 4 * h + 2 + i), ("u", 5, 4 * h + i)):
                add_up(t, way, d, ch, False)
                give(t, way, d, ch)

    def step(t, n, quarter_d, quarter_u):
        mate_there(t, quarter_d // 2, n, 8 - n)
        for i in range(2):
            for way, d, ch in (("d", n, 2 * quarter_d + i), ("u", 8 - n, 2 * quarter_u + i)):
                back = d + 1 if way == "d" else d - 1
                sent[t, "r" + way, back, ch].wait_recv()
                add_up(t, way, d, ch, True)
                give(t, way, d, ch)

    def scatter_last(t, ch, own):
        mate_there(t, ch // 4, 0)
        sent[t, "rd", 1, ch].wait_recv()
        sent[t, "ru", 7, ch].wait_recv()
        at = rows(ch, FINE)
        tot[t, at] = (
            own[at].astype(F32)
            + (part[t, 0, 0, at].astype(F32) + l_core[t, 0, at].astype(F32))
            + (l_down[t, 0, at].astype(F32) + l_up[t, 0, at].astype(F32))
        ).astype(BF)

    def each(body, first=0, last=RING):
        def turn(k, carry):
            body(k)
            return carry

        lax.fori_loop(first, last, turn, 0)

    both = ((0, 0), (1, 1))
    for ch in range(2):
        entered(("a", ch))
        gather_first("a", xg0, ch, 2)
    entered("t")
    table_step(0)
    for d in (1, 2, 3, 4):
        gather_step("a", xg0, d, both, 2)
        table_step(d)
        if d == 3:
            entered("x1")
            for ch in range(2):
                gather_first("x1", x1, ch, 2)
    tables_there()
    places(0, None, pos_full, post_full)
    for h in range(2):
        places(1, h, pos_half.at[h], post_half.at[h])
    for d in range(RING):
        gathered("a", xg0, d)
    gather_step("x1", x1, 1, both, 2)

    def pick0(k):
        pick(None, xg0[k, :, 0], xg, k)
        pick(None, xg0[k, :, 1], gg, k)
        pick_scales(0, None, k)

    each(pick0)
    gather_step("x1", x1, 2, both, 2)
    for w in ("wg", "wu", "wd"):
        entered((w, 0))
    pre(0, 0)
    gather_step("x1", x1, 3, both, 2)
    for u0 in (0, 4):
        post_rows(0, 0, 0, u0, 4)
    gather_step("x1", x1, 4, both, 2)
    for d in range(RING):
        gathered("x1", x1, d)
    entered(("wg", 1))
    entered(("wu", 1))
    pre(0, 1)

    def pick1(h):
        each(lambda k: pick(h, x1[k, :, half(h)], xg, k))

    pick1(0)
    for h in range(2):
        each(lambda k: pick_scales(1, h, k))
    entered(("wd", 1))

    def finish(t, h, ds):
        for d in ds:
            put(t, halved(t, h, d), PLACE[d])
            give_mate(t, h, d)

    post_rows(0, 0, 1, 5, 3)
    finish(0, 0, (4, 3, 5))
    for h in range(2):
        far(0, h)
        near(0, h)
    post_rows(0, 0, 1, 3, 2)
    finish(0, 0, (2, 6))
    post_rows(0, 0, 1, 0, 3)
    finish(0, 0, (1, 7, 0))
    step(0, 3, 0, 1)
    pre(0, 0)
    step(0, 2, 1, 0)
    step(0, 3, 2, 3)
    pre(0, 1)
    step(0, 2, 0, 1)
    step(0, 2, 3, 2)
    pick1(1)
    pre(1, 0)
    step(0, 1, 0, 0)
    step(0, 1, 1, 1)
    step(0, 2, 2, 3)
    pre(1, 1)
    step(0, 1, 3, 2)

    def passing(quarter):
        for ch in (2 * quarter, 2 * quarter + 1):
            scatter_last(0, ch, xg0.at[0, 0, 1])
            at = rows(ch, FINE)
            send(("pass", ch), tot.at[0, at], g1.at[0, 0, at], pass_to, "pass")

    def passed(quarter):
        for ch in (2 * quarter, 2 * quarter + 1):
            sent["pass", ch].wait_recv()
            gather_first("g1", g1, ch, FINE)

    passing(0)
    passing(1)
    step(0, 1, 2, 3)
    passed(0)
    passed(1)
    passing(2)
    passing(3)

    def level(d, h, i):
        up, down = 4 * h + 2 * i, 4 * h + 2 - 2 * i
        gather_step("g1", g1, d, ((up, down), (up + 1, down + 1)), FINE)

    def take(h, ds):
        for d in ds:
            gathered("g1", g1, d, h, half(h))
            pick(h, g1[PLACE[d], :, half(h)], gg, PLACE[d])

    level(1, 0, 0)
    level(1, 0, 1)
    take(0, (0,))
    passed(2)
    passed(3)
    level(2, 0, 0)
    level(2, 0, 1)
    take(0, (1, 7))
    level(1, 1, 0)
    level(1, 1, 1)
    take(0, (2, 6))
    post_rows(1, 0, 0, 0, 5)
    level(3, 0, 0)
    level(3, 0, 1)
    post_rows(1, 0, 1, 0, 5)
    level(2, 1, 0)
    take(0, (3, 5))
    post_rows(1, 0, 0, 5, 2)
    level(2, 1, 1)
    post_rows(1, 0, 1, 5, 2)
    level(4, 0, 0)
    finish(1, 0, (3, 5))
    level(3, 1, 0)
    take(0, (4,))
    post_rows(1, 0, 0, 7, 1)
    level(3, 1, 1)
    near(1, 0)
    post_rows(1, 0, 1, 7, 1)
    finish(1, 0, (4, 2, 6))
    level(4, 1, 0)
    far(1, 0)
    finish(1, 0, (1, 7, 0))
    take(1, (4, 3, 5))
    step(1, 2, 1, 0)
    post_rows(1, 1, 0, 5, 3)
    step(1, 3, 0, 1)
    post_rows(1, 1, 1, 5, 3)
    finish(1, 1, (4, 3, 5))
    step(1, 2, 0, 1)
    far(1, 1)
    near(1, 1)
    def final(quarter):
        for ch in (2 * quarter, 2 * quarter + 1):
            scatter_last(1, ch, g1.at[0, 0])
        at = rows(quarter, 4)
        enter(("fin", quarter), [(tot.at[1, at], out_ref.at[at])], out_ref.at[at])

    take(1, (2, 6))
    post_rows(1, 1, 0, 3, 2)
    post_rows(1, 1, 1, 3, 2)
    finish(1, 1, (2, 6))
    step(1, 1, 0, 0)
    step(1, 3, 2, 3)
    take(1, (0, 1, 7))
    step(1, 2, 3, 2)
    post_rows(1, 1, 0, 0, 3)
    step(1, 1, 1, 1)
    post_rows(1, 1, 1, 0, 3)
    step(1, 2, 2, 3)
    finish(1, 1, (1, 7, 0))
    final(0)
    step(1, 1, 3, 2)
    final(1)
    step(1, 1, 2, 3)
    final(2)
    final(3)
    for quarter in range(4):
        entered(("fin", quarter))

    for name, buf in (("a", xg0), ("x1", x1), ("g1", g1), ("t", tab)):
        group = ("t", "c") if name == "t" else (name, "c", 0, 0)
        make((name, "z"), group, buf.at[0:7, 0], buf.at[0:7, 1], z_up).wait_send()
        make((name, "c"), group, buf.at[:, 0], buf.at[:, 1], mate).wait_send()
    for t in range(2):
        make((t, "rz"), (t, "rc", 0, 0), part.at[t, 0:7, 0], part.at[t, 0:7, 0], z_up).wait_send()
        make((t, "rc"), (t, "rc", 0, 0), part.at[t, :, 1], part.at[t, :, 1], mate).wait_send()
    make("pass", ("pass", 0), tot.at[0], tot.at[0], pass_to).wait_send()

    @pl.when(mixed)
    def _():
        for key, whole in ends:
            make(key, key, whole, whole, swap).wait_send()

    assert len(senders) <= SENDERS and len(takers) <= TAKERS, (len(senders), len(takers))

def shards(grad_out, saved_inputs, routes, gate_weights, w_gate, w_up, w_down):
    block = pltpu.VMEM((RING, 2, TOK, D), BF)
    return pl.pallas_call(
        kernel,
        out_shape=jax.ShapeDtypeStruct((TOK, D), BF),
        in_specs=[pl.BlockSpec(memory_space=pl.ANY)] * 7,
        out_specs=pl.BlockSpec(memory_space=pl.ANY),
        scratch_shapes=[
            pltpu.VMEM((RING, 2, 2, TOK, D), BF),
            block, block,
            pltpu.VMEM((RING, 2, 2, 16, TOK), F32),
            pltpu.VMEM((2, D, H), BF),
            pltpu.VMEM((2, D, H), BF),
            pltpu.VMEM((2, H, D), BF),
            pltpu.VMEM((2, RING, 2, TOK, D), BF),
            pltpu.VMEM((2, RING, TOK, D), BF),
            pltpu.VMEM((2, 4, TOK, D), BF),
            pltpu.VMEM((2, 4, TOK, D), BF),
            pltpu.VMEM((2, TOK, D), BF),
            pltpu.VMEM((2, RING * CAP, D), BF),
            pltpu.VMEM((2, RING * CAP, D), BF),
            pltpu.VMEM((2, 2, RING * CAP, H), F32),
            pltpu.VMEM((2, 2, RING * CAP, H), F32),
            pltpu.VMEM((RING, 2 * CAP, D), BF),
            pltpu.VMEM((3, 2, RING * CAP, 1), F32),
            pltpu.VMEM((16, 256), F32),
            pltpu.VMEM((RING, 256, 2), F32),
            pltpu.VMEM((2, 16, 128), F32),
            pltpu.VMEM((2, RING, 128, 2), F32),
            pltpu.VMEM((2, 8, TOK), jnp.int32),
            pltpu.VMEM((2, 16, TOK), F32),
            pltpu.SemaphoreType.DMA((SENDERS,)),
            pltpu.SemaphoreType.DMA((TAKERS,)),
            pltpu.SemaphoreType.DMA((20,)),
        ],
        compiler_params=pltpu.CompilerParams(
            collective_id=0, has_side_effects=True, vmem_limit_bytes=63 << 20
        ),
        name="moe_back",
    )(
        grad_out[0],
        saved_inputs[0],
        jnp.swapaxes(routes[0], 1, 2),
        jnp.swapaxes(gate_weights[0], 1, 2),
        w_gate[0],
        w_up[0],
        w_down[0],
    )[None]


def solution(mesh):
    placed = (
        P("section", "expert", None),
        P("section", None, "expert", None),
        P("section", None, "expert", None),
        P("section", None, "expert", None),
        P("section", "expert", None, None),
        P("section", "expert", None, None),
        P("section", "expert", None, None),
    )
    return jax.shard_map(
        shards, mesh=mesh, in_specs=placed, out_specs=P("section", "expert", None), check_vma=False
    )
```

```python
import jax
import jax.numpy as jnp
from jax import lax
from jax.experimental import pallas as pl
from jax.experimental.pallas import tpu as pltpu
from jax.sharding import PartitionSpec as P

BF = jnp.bfloat16
F32 = jnp.float32
TOK = 128
D = 1024
H = 512
CAP = 80
RING = 8
PLACE = {0: 0, 1: 1, 7: 2, 2: 3, 6: 4, 3: 5, 5: 6, 4: 7}
SENDERS = 40
TAKERS = 166
FINE = 8


def nt(a, b):
    return lax.dot_general(a, b, (((1,), (1,)), ((), ())), preferred_element_type=F32)


def nn(a, b):
    return lax.dot_general(a, b, (((1,), (0,)), ((), ())), preferred_element_type=F32)


def kernel(
    grad_in, saved_in, routes_in, weights_in, wg_in, wu_in, wd_in, out_ref,
    xg0, x1, g1, tab, wg, wu, wd, part, l_core, l_down, l_up, tot,
    xg, gg, gp, up, rw, ws, pos_full, post_full, pos_half, post_half, own_routes, own_table, ssem, rsem, lsem,
):
    s = lax.axis_index("section")
    e = lax.axis_index("expert")
    core = lax.rem(s, 2)
    x_lo = lax.rem(e, 2)
    mixed = core != x_lo
    other_core = s + 1 - 2 * core
    other_x = e + 1 - 2 * x_lo
    z_up = (s, lax.rem(e + 2, 16))
    z_down = (s, lax.rem(e + 14, 16))
    mate = (other_core, e)
    swap = (other_core, other_x)
    pass_to = (lax.rem(s + 16 - 2 * (1 - x_lo), 16), other_x)
    pass_from = (lax.rem(s + 2 * x_lo, 16), other_x)
    home = lax.select(mixed, other_x, e)

    barrier = pltpu.get_barrier_semaphore()
    for peer in (z_up, z_down, mate, swap, pass_to, pass_from):
        pl.semaphore_signal(barrier, inc=1, device_id=peer, device_id_type=pl.DeviceIdType.MESH)

    senders, takers, sent, ends = {}, {}, {}, []

    def number(table, key):
        return table.setdefault(key, len(table))

    def make(batch, group, src, dst, peer):
        if group[0] == 1:
            group = (0,) + group[1:]
        elif group[0] == "g1" and group[1] == "c":
            group = ("a",) + group[1:]
        elif group[0] == "g1":
            place = 4 if group[2] == 3 else 3 - group[2]
            group = (0, "r" + group[1], place if group[1] == "d" else 8 - place, group[3])
        return pltpu.make_async_remote_copy(
            src_ref=src, dst_ref=dst,
            send_sem=ssem.at[number(senders, batch)], recv_sem=rsem.at[number(takers, group)],
            device_id=peer, device_id_type=pl.DeviceIdType.MESH,
        )

    def send(key, src, dst, peer, batch):
        sent[key] = make(batch, key, src, dst, peer)
        sent[key].start()

    moves = {}

    def enter(key, pairs, whole):
        i = number(moves, key)

        @pl.when(jnp.logical_not(mixed))
        def _():
            for src, dst in pairs:
                pltpu.make_async_copy(src, dst, lsem.at[i]).start()

        @pl.when(mixed)
        def _():
            for src, dst in pairs:
                make(key, key, src, dst, swap).start()

        ends.append((key, whole))

    def entered(key):
        whole = dict(ends)[key]

        @pl.when(jnp.logical_not(mixed))
        def _():
            pltpu.make_async_copy(whole, whole, lsem.at[moves[key]]).wait()

        @pl.when(mixed)
        def _():
            make(key, key, whole, whole, swap).wait_recv()

    loads = [
        pltpu.make_async_copy(routes_in, own_routes, lsem.at[18]),
        pltpu.make_async_copy(weights_in, own_table.at[:, 8:16], lsem.at[19]),
    ]
    for load in loads:
        load.start()
    pl.semaphore_wait(barrier, 6)
    for ch in range(2):
        at = pl.ds(64 * ch, 64)
        enter(
            ("a", ch),
            [
                (saved_in.at[0, at], xg0.at[0, 0, 0, at]),
                (grad_in.at[at], xg0.at[0, 0, 1, at]),
            ],
            xg0.at[0, 0, :, at],
        )
    for load in loads:
        load.wait()
    own_table[:, 0:8] = own_routes[...].astype(F32)
    enter("t", [(own_table, tab.at[0, 0])], tab.at[0, 0])
    for j in range(2):
        for name, src, dst in (("wg", wg_in, wg), ("wu", wu_in, wu), ("wd", wd_in, wd)):
            enter((name, j), [(src.at[j], dst.at[j])], dst.at[j])
        if j == 0:
            enter("x1", [(saved_in.at[1], x1.at[0, 0])], x1.at[0, 0])

    def rows(ch, n):
        return pl.ds(TOK // n * ch, TOK // n)

    def upper(ch, n):
        return ch % 2 == 0 if n == 2 else ch // 2 % 2 == 0

    def piece(buf, k, c, at):
        return buf.at[k, c, :, at] if len(buf.shape) == 5 else buf.at[k, c, at]

    def to_mate(name, buf, d, ch, n):
        k = PLACE[d]
        at = rows(ch, n)
        group = (name, "c", d, 2 * ch // n if n == FINE else 0)
        make((name, "c"), group, piece(buf, k, 0, at), piece(buf, k, 1, at), mate).start()

    def gathered(name, buf, d, h=0, at=pl.ds(0, TOK)):
        k = PLACE[d]
        group = (name, "c", d, h)
        make((name, "c"), group, piece(buf, k, 0, at), piece(buf, k, 1, at), mate).wait_recv()

    def hop(name, buf, way, d, ch, n):
        src, dst = (d, d + 1) if way == "u" else ((8 - d) % 8, 7 - d)
        at = rows(ch, n)
        send(
            (name, way, d, ch),
            piece(buf, PLACE[src], 0, at),
            piece(buf, PLACE[dst], 0, at),
            z_up if way == "u" else z_down,
            (name, "z"),
        )

    def gather_first(name, buf, ch, n):
        hop(name, buf, "u", 0, ch, n)
        hop(name, buf, "d", 0, ch, n)
        to_mate(name, buf, 0, ch, n)

    def gather_step(name, buf, d, chs, n):
        for pair in chs:
            for way, ch in zip("ud", pair):
                here = d if way == "u" else 8 - d
                half = (way == "u") == upper(ch, n)
                if d < 4 or half:
                    sent[name, way, d - 1, ch].wait_recv()
                    if d < 3 or (d == 3 and half):
                        hop(name, buf, way, d, ch, n)
                    to_mate(name, buf, here, ch, n)

    def table_step(d):
        def on(way, d, k, to, peer):
            send(("t", way, d), tab.at[k, 0], tab.at[to, 0], peer, ("t", "z"))

        def across(d, k):
            make(("t", "c"), ("t", "c"), tab.at[k, 0], tab.at[k, 1], mate).start()

        if d == 0:
            on("u", 0, 0, PLACE[1], z_up)
            on("d", 0, 0, PLACE[7], z_down)
            across(0, 0)
            return
        sent["t", "u", d - 1].wait_recv()
        k = PLACE[d]
        if d < 4:
            on("u", d, k, PLACE[d + 1], z_up)
        across(d, k)
        if d < 4:
            sent["t", "d", d - 1].wait_recv()
            k = PLACE[8 - d]
            if d < 3:
                on("d", d, k, PLACE[7 - d], z_down)
            across(8 - d, k)

    def tables_there():
        make(("t", "c"), ("t", "c"), tab.at[:, 0], tab.at[:, 1], mate).wait_recv()

    def half(h):
        return pl.ds(0, TOK) if h is None else pl.ds(64 * h, 64)

    def lanes(k, t, h, first):
        both = [tab[k, c, t, first : first + 8] for c in range(2)]
        if h is not None:
            both = [v[:, 64 * h : 64 * h + 64] for v in both]
        return jnp.concatenate(both, axis=1)

    def places(t, h, pos, post):
        masks = []
        for k in range(RING):
            named = lanes(k, t, h, 0)
            for j in range(2):
                hit = named == (2 * home + j).astype(F32)
                masks.append(jnp.sum(jnp.where(hit, 1.0, 0.0), axis=0, keepdims=True))
        mask = jnp.concatenate(masks, axis=0)
        n = mask.shape[1]
        before = lax.broadcasted_iota(jnp.int32, (n, n), 0) < lax.broadcasted_iota(
            jnp.int32, (n, n), 1
        )
        earlier = nn(mask.astype(BF), jnp.where(before, 1.0, 0.0).astype(BF))
        where = jnp.where(mask > 0.5, earlier, -1000.0)
        pos[...] = where
        turned = jnp.transpose(jnp.concatenate([where, jnp.zeros((112, n), F32)], axis=0))
        for k in range(RING):
            post[k] = turned[:, 2 * k : 2 * k + 2]

    def chosen(pos, k):
        slot = lax.broadcasted_iota(jnp.int32, (CAP, pos.shape[1]), 0).astype(F32)
        return [slot == pos[pl.ds(2 * k + j, 1)] for j in range(2)]

    def unit_rows(k):
        return pl.ds(pl.multiple_of(k * CAP, 16), CAP)

    def pos_of(h):
        return pos_full if h is None else pos_half.at[h]

    def pick(h, tokens, dst, k):
        pos = pos_of(h)
        hot = jnp.concatenate([jnp.where(c, 1.0, 0.0) for c in chosen(pos, k)], axis=0).astype(BF)
        got = nn(hot, tokens.reshape(pos.shape[1], D)).astype(BF)
        dst[0, unit_rows(k)] = got[:CAP]
        dst[1, unit_rows(k)] = got[CAP:]

    def pick_scales(t, h, k):
        named = lanes(k, t, h, 0)
        weight = lanes(k, t, h, 8)
        for j, hit in enumerate(chosen(pos_of(h), k)):
            mine = jnp.sum(
                jnp.where(named == (2 * home + j).astype(F32), weight, 0.0), axis=0, keepdims=True
            )
            ws[t + (h or 0), j, unit_rows(k)] = jnp.sum(jnp.where(hit, mine, 0.0), axis=1, keepdims=True)

    def pre(h, j):
        x = xg[j]
        gp[h, j] = nn(x, wg[j])
        up[h, j] = nn(x, wu[j])

    def post_rows(t, h, j, k0, n):
        at = pl.ds(k0 * CAP, n * CAP)
        hidden = nt(gg[j, at], wd[j])
        gate = gp[h, j, at]
        sig = 1.0 / (1.0 + jnp.exp(-gate))
        hs = hidden * sig
        gate_grad = (hs * up[h, j, at] * (1.0 + gate * (1.0 - sig))).astype(BF)
        up_grad = (hs * gate).astype(BF)
        grown = nt(gate_grad, wg[j]) + nt(up_grad, wu[j])
        grown = (grown * ws[t + h, j, at]).astype(BF)
        for i in range(n):
            rw[k0 + i, j * CAP : (j + 1) * CAP] = grown[i * CAP : (i + 1) * CAP]

    def put(t, h, k):
        col = post_full[k] if h is None else post_half[h, k]
        lane = lax.broadcasted_iota(jnp.int32, (col.shape[0], 2 * CAP), 1).astype(F32)
        hot = jnp.logical_or(lane == col[:, 0:1], lane == col[:, 1:2] + float(CAP))
        summed = nn(jnp.where(hot, 1.0, 0.0).astype(BF), rw[k]).astype(BF)
        part[t, k, :, half(h)] = summed.reshape(2, col.shape[0] // 2, D)

    def halved(t, h, d):
        return h if t == 1 else None

    def give_mate(t, h, d):
        k = PLACE[d]
        h = halved(t, h, d)
        at = half(h)
        send((t, "rc", d, h or 0), part.at[t, k, 1, at], l_core.at[t, k, at], mate, (t, "rc"))

    there = set()

    def mate_there(t, h, *ds):
        for d in ds:
            key = (t, "rc", d, halved(t, h, d) or 0)
            if key not in there:
                there.add(key)
                sent[key].wait_recv()

    def give(t, way, d, ch):
        src = part.at[t, PLACE[d], 0, rows(ch, FINE)]
        if way == "d":
            send((t, "rd", d, ch), src, l_down.at[t, d - 1, rows(ch, FINE)], z_down, (t, "rz"))
        else:
            send((t, "ru", d, ch), src, l_up.at[t, 7 - d, rows(ch, FINE)], z_up, (t, "rz"))

    def add_up(t, way, d, ch, arrived):
        k = PLACE[d]
        at = rows(ch, FINE)
        value = part[t, k, 0, at].astype(F32) + l_core[t, k, at].astype(F32)
        if arrived:
            landed = l_down[t, d, at] if way == "d" else l_up[t, 8 - d, at]
            value = value + landed.astype(F32)
        part[t, k, 0, at] = value.astype(BF)

    def far(t, h):
        mate_there(t, h, 4)
        for i in range(2):
            for way, ch in (("d", 4 * h + i), ("u", 4 * h + 2 + i)):
                add_up(t, way, 4, ch, False)
                give(t, way, 4, ch)

    def near(t, h):
        mate_there(t, h, 3, 5)
        for i in range(2):
            for way, d, ch in (("d", 3, 4 * h + 2 + i), ("u", 5, 4 * h + i)):
                add_up(t, way, d, ch, False)
                give(t, way, d, ch)

    def step(t, n, quarter_d, quarter_u):
        mate_there(t, quarter_d // 2, n, 8 - n)
        for i in range(2):
            for way, d, ch in (("d", n, 2 * quarter_d + i), ("u", 8 - n, 2 * quarter_u + i)):
                back = d + 1 if way == "d" else d - 1
                sent[t, "r" + way, back, ch].wait_recv()
                add_up(t, way, d, ch, True)
                give(t, way, d, ch)

    def scatter_last(t, ch, own):
        mate_there(t, ch // 4, 0)
        sent[t, "rd", 1, ch].wait_recv()
        sent[t, "ru", 7, ch].wait_recv()
        at = rows(ch, FINE)
        tot[t, at] = (
            own[at].astype(F32)
            + (part[t, 0, 0, at].astype(F32) + l_core[t, 0, at].astype(F32))
            + (l_down[t, 0, at].astype(F32) + l_up[t, 0, at].astype(F32))
        ).astype(BF)

    def each(body, first=0, last=RING):
        def turn(k, carry):
            body(k)
            return carry

        lax.fori_loop(first, last, turn, 0)

    both = ((0, 0), (1, 1))
    for ch in range(2):
        entered(("a", ch))
        gather_first("a", xg0, ch, 2)
    entered("t")
    table_step(0)
    for d in (1, 2, 3, 4):
        gather_step("a", xg0, d, both, 2)
        table_step(d)
        if d == 3:
            entered("x1")
            for ch in range(2):
                gather_first("x1", x1, ch, 2)
    tables_there()
    places(0, None, pos_full, post_full)
    for h in range(2):
        places(1, h, pos_half.at[h], post_half.at[h])
    for d in range(RING):
        gathered("a", xg0, d)
    gather_step("x1", x1, 1, both, 2)

    def pick0(k):
        pick(None, xg0[k, :, 0], xg, k)
        pick(None, xg0[k, :, 1], gg, k)
        pick_scales(0, None, k)

    each(pick0)
    gather_step("x1", x1, 2, both, 2)
    for w in ("wg", "wu", "wd"):
        entered((w, 0))
    pre(0, 0)
    gather_step("x1", x1, 3, both, 2)
    for u0 in (0, 4):
        post_rows(0, 0, 0, u0, 4)
    gather_step("x1", x1, 4, both, 2)
    for d in range(RING):
        gathered("x1", x1, d)
    entered(("wg", 1))
    entered(("wu", 1))
    pre(0, 1)

    def pick1(h):
        each(lambda k: pick(h, x1[k, :, half(h)], xg, k))

    pick1(0)
    for h in range(2):
        each(lambda k: pick_scales(1, h, k))
    entered(("wd", 1))

    def finish(t, h, ds):
        for d in ds:
            put(t, halved(t, h, d), PLACE[d])
            give_mate(t, h, d)

    post_rows(0, 0, 1, 5, 3)
    finish(0, 0, (4, 3, 5))
    for h in range(2):
        far(0, h)
        near(0, h)
    post_rows(0, 0, 1, 3, 2)
    finish(0, 0, (2, 6))
    post_rows(0, 0, 1, 0, 3)
    finish(0, 0, (1, 7, 0))
    step(0, 3, 0, 1)
    pre(0, 0)
    step(0, 2, 1, 0)
    step(0, 3, 2, 3)
    pre(0, 1)
    step(0, 2, 0, 1)
    step(0, 2, 3, 2)
    pick1(1)
    pre(1, 0)
    step(0, 1, 0, 0)
    step(0, 1, 1, 1)
    step(0, 2, 2, 3)
    pre(1, 1)
    step(0, 1, 3, 2)

    def passing(quarter):
        for ch in (2 * quarter, 2 * quarter + 1):
            scatter_last(0, ch, xg0.at[0, 0, 1])
            at = rows(ch, FINE)
            send(("pass", ch), tot.at[0, at], g1.at[0, 0, at], pass_to, "pass")

    def passed(quarter):
        for ch in (2 * quarter, 2 * quarter + 1):
            sent["pass", ch].wait_recv()
            gather_first("g1", g1, ch, FINE)

    passing(0)
    passing(1)
    step(0, 1, 2, 3)
    passed(0)
    passed(1)
    passing(2)
    passing(3)

    def level(d, h, i):
        up, down = 4 * h + 2 * i, 4 * h + 2 - 2 * i
        gather_step("g1", g1, d, ((up, down), (up + 1, down + 1)), FINE)

    def take(h, ds):
        for d in ds:
            gathered("g1", g1, d, h, half(h))
            pick(h, g1[PLACE[d], :, half(h)], gg, PLACE[d])

    level(1, 0, 0)
    level(1, 0, 1)
    take(0, (0,))
    passed(2)
    passed(3)
    level(2, 0, 0)
    level(2, 0, 1)
    take(0, (1, 7))
    level(1, 1, 0)
    level(1, 1, 1)
    take(0, (2, 6))
    post_rows(1, 0, 0, 0, 5)
    level(3, 0, 0)
    level(3, 0, 1)
    post_rows(1, 0, 1, 0, 5)
    level(2, 1, 0)
    take(0, (3, 5))
    post_rows(1, 0, 0, 5, 2)
    level(2, 1, 1)
    post_rows(1, 0, 1, 5, 2)
    level(4, 0, 0)
    finish(1, 0, (3, 5))
    level(3, 1, 0)
    take(0, (4,))
    post_rows(1, 0, 0, 7, 1)
    level(3, 1, 1)
    near(1, 0)
    post_rows(1, 0, 1, 7, 1)
    finish(1, 0, (4, 2, 6))
    level(4, 1, 0)
    far(1, 0)
    take(1, (3, 5, 4))
    step(1, 2, 1, 0)
    post_rows(1, 1, 0, 5, 3)
    post_rows(1, 1, 1, 5, 3)
    step(1, 3, 0, 1)
    finish(1, 1, (4, 3, 5))
    finish(1, 0, (1, 7, 0))
    far(1, 1)
    step(1, 2, 0, 1)
    near(1, 1)

    def final(quarter):
        for ch in (2 * quarter, 2 * quarter + 1):
            scatter_last(1, ch, g1.at[0, 0])
            at = rows(ch, FINE)
            enter(("fin", ch), [(tot.at[1, at], out_ref.at[at])], out_ref.at[at])

    take(1, (2, 6))
    post_rows(1, 1, 0, 3, 2)
    post_rows(1, 1, 1, 3, 2)
    finish(1, 1, (2, 6))
    step(1, 3, 2, 3)
    step(1, 1, 0, 0)
    take(1, (0, 1, 7))
    step(1, 2, 3, 2)
    post_rows(1, 1, 0, 0, 3)
    step(1, 2, 2, 3)
    step(1, 1, 1, 1)
    post_rows(1, 1, 1, 0, 3)
    finish(1, 1, (1, 7, 0))
    final(0)
    step(1, 1, 2, 2)
    final(1)
    step(1, 1, 3, 3)
    final(2)
    final(3)
    for ch in range(FINE):
        entered(("fin", ch))

    for name, buf in (("a", xg0), ("x1", x1), ("g1", g1), ("t", tab)):
        group = ("t", "c") if name == "t" else (name, "c", 0, 0)
        make((name, "z"), group, buf.at[0:7, 0], buf.at[0:7, 1], z_up).wait_send()
        make((name, "c"), group, buf.at[:, 0], buf.at[:, 1], mate).wait_send()
    for t in range(2):
        make((t, "rz"), (t, "rc", 0, 0), part.at[t, 0:7, 0], part.at[t, 0:7, 0], z_up).wait_send()
        make((t, "rc"), (t, "rc", 0, 0), part.at[t, :, 1], part.at[t, :, 1], mate).wait_send()
    make("pass", ("pass", 0), tot.at[0], tot.at[0], pass_to).wait_send()

    @pl.when(mixed)
    def _():
        for key, whole in ends:
            make(key, key, whole, whole, swap).wait_send()

    assert len(senders) <= SENDERS and len(takers) <= TAKERS, (len(senders), len(takers))

def shards(grad_out, saved_inputs, routes, gate_weights, w_gate, w_up, w_down):
    block = pltpu.VMEM((RING, 2, TOK, D), BF)
    return pl.pallas_call(
        kernel,
        out_shape=jax.ShapeDtypeStruct((TOK, D), BF),
        in_specs=[pl.BlockSpec(memory_space=pl.ANY)] * 7,
        out_specs=pl.BlockSpec(memory_space=pl.ANY),
        scratch_shapes=[
            pltpu.VMEM((RING, 2, 2, TOK, D), BF),
            block, block,
            pltpu.VMEM((RING, 2, 2, 16, TOK), F32),
            pltpu.VMEM((2, D, H), BF),
            pltpu.VMEM((2, D, H), BF),
            pltpu.VMEM((2, H, D), BF),
            pltpu.VMEM((2, RING, 2, TOK, D), BF),
            pltpu.VMEM((2, RING, TOK, D), BF),
            pltpu.VMEM((2, 4, TOK, D), BF),
            pltpu.VMEM((2, 4, TOK, D), BF),
            pltpu.VMEM((2, TOK, D), BF),
            pltpu.VMEM((2, RING * CAP, D), BF),
            pltpu.VMEM((2, RING * CAP, D), BF),
            pltpu.VMEM((2, 2, RING * CAP, H), F32),
            pltpu.VMEM((2, 2, RING * CAP, H), F32),
            pltpu.VMEM((RING, 2 * CAP, D), BF),
            pltpu.VMEM((3, 2, RING * CAP, 1), F32),
            pltpu.VMEM((16, 256), F32),
            pltpu.VMEM((RING, 256, 2), F32),
            pltpu.VMEM((2, 16, 128), F32),
            pltpu.VMEM((2, RING, 128, 2), F32),
            pltpu.VMEM((2, 8, TOK), jnp.int32),
            pltpu.VMEM((2, 16, TOK), F32),
            pltpu.SemaphoreType.DMA((SENDERS,)),
            pltpu.SemaphoreType.DMA((TAKERS,)),
            pltpu.SemaphoreType.DMA((20,)),
        ],
        compiler_params=pltpu.CompilerParams(
            collective_id=0, has_side_effects=True, vmem_limit_bytes=63 << 20
        ),
        name="moe_back",
    )(
        grad_out[0],
        saved_inputs[0],
        jnp.swapaxes(routes[0], 1, 2),
        jnp.swapaxes(gate_weights[0], 1, 2),
        w_gate[0],
        w_up[0],
        w_down[0],
    )[None]


def solution(mesh):
    placed = (
        P("section", "expert", None),
        P("section", None, "expert", None),
        P("section", None, "expert", None),
        P("section", None, "expert", None),
        P("section", "expert", None, None),
        P("section", "expert", None, None),
        P("section", "expert", None, None),
    )
    return jax.shard_map(
        shards, mesh=mesh, in_specs=placed, out_specs=P("section", "expert", None), check_vma=False
    )
```

```python
import jax
import jax.numpy as jnp
from jax import lax
from jax.experimental import pallas as pl
from jax.experimental.pallas import tpu as pltpu
from jax.sharding import PartitionSpec as P

BF = jnp.bfloat16
F32 = jnp.float32
TOK = 128
D = 1024
H = 512
CAP = 80
RING = 8
PLACE = {0: 0, 1: 1, 7: 2, 2: 3, 6: 4, 3: 5, 5: 6, 4: 7}
SENDERS = 40
TAKERS = 166
FINE = 8


def nt(a, b):
    return lax.dot_general(a, b, (((1,), (1,)), ((), ())), preferred_element_type=F32)


def nn(a, b):
    return lax.dot_general(a, b, (((1,), (0,)), ((), ())), preferred_element_type=F32)


def kernel(
    grad_in, saved_in, routes_in, weights_in, wg_in, wu_in, wd_in, out_ref,
    xg0, x1, g1, tab, wg, wu, wd, part, l_core, l_down, l_up, tot,
    xg, gg, gp, up, rw, ws, pos_full, post_full, pos_half, post_half, own_routes, own_table, ssem, rsem, lsem,
):
    s = lax.axis_index("section")
    e = lax.axis_index("expert")
    core = lax.rem(s, 2)
    x_lo = lax.rem(e, 2)
    mixed = core == x_lo
    other_core = s + 1 - 2 * core
    other_x = e + 1 - 2 * x_lo
    z_up = (s, lax.rem(e + 2, 16))
    z_down = (s, lax.rem(e + 14, 16))
    mate = (other_core, e)
    swap = (other_core, other_x)
    pass_to = (lax.rem(s + 16 - 2 * x_lo, 16), other_x)
    pass_from = (lax.rem(s + 2 * (1 - x_lo), 16), other_x)
    home = lax.select(mixed, other_x, e)

    barrier = pltpu.get_barrier_semaphore()
    for peer in (z_up, z_down, mate, swap, pass_to, pass_from):
        pl.semaphore_signal(barrier, inc=1, device_id=peer, device_id_type=pl.DeviceIdType.MESH)

    senders, takers, sent, ends = {}, {}, {}, []

    def number(table, key):
        return table.setdefault(key, len(table))

    def make(batch, group, src, dst, peer):
        if group[0] == 1:
            group = (0,) + group[1:]
        elif group[0] == "g1" and group[1] == "c":
            group = ("a",) + group[1:]
        elif group[0] == "g1":
            place = 4 if group[2] == 3 else 3 - group[2]
            group = (0, "r" + group[1], place if group[1] == "d" else 8 - place, group[3])
        return pltpu.make_async_remote_copy(
            src_ref=src, dst_ref=dst,
            send_sem=ssem.at[number(senders, batch)], recv_sem=rsem.at[number(takers, group)],
            device_id=peer, device_id_type=pl.DeviceIdType.MESH,
        )

    def send(key, src, dst, peer, batch):
        sent[key] = make(batch, key, src, dst, peer)
        sent[key].start()

    moves = {}

    def enter(key, pairs, whole):
        i = number(moves, key)

        @pl.when(jnp.logical_not(mixed))
        def _():
            for src, dst in pairs:
                pltpu.make_async_copy(src, dst, lsem.at[i]).start()

        @pl.when(mixed)
        def _():
            for src, dst in pairs:
                make(key, key, src, dst, swap).start()

        ends.append((key, whole))

    def entered(key):
        whole = dict(ends)[key]

        @pl.when(jnp.logical_not(mixed))
        def _():
            pltpu.make_async_copy(whole, whole, lsem.at[moves[key]]).wait()

        @pl.when(mixed)
        def _():
            make(key, key, whole, whole, swap).wait_recv()

    loads = [
        pltpu.make_async_copy(routes_in, own_routes, lsem.at[18]),
        pltpu.make_async_copy(weights_in, own_table.at[:, 8:16], lsem.at[19]),
    ]
    for load in loads:
        load.start()
    pl.semaphore_wait(barrier, 6)
    for ch in range(2):
        at = pl.ds(64 * ch, 64)
        enter(
            ("a", ch),
            [
                (saved_in.at[0, at], xg0.at[0, 0, 0, at]),
                (grad_in.at[at], xg0.at[0, 0, 1, at]),
            ],
            xg0.at[0, 0, :, at],
        )
    for load in loads:
        load.wait()
    own_table[:, 0:8] = own_routes[...].astype(F32)
    enter("t", [(own_table, tab.at[0, 0])], tab.at[0, 0])
    for j in range(2):
        for name, src, dst in (("wg", wg_in, wg), ("wu", wu_in, wu), ("wd", wd_in, wd)):
            enter((name, j), [(src.at[j], dst.at[j])], dst.at[j])
        if j == 0:
            enter("x1", [(saved_in.at[1], x1.at[0, 0])], x1.at[0, 0])

    def rows(ch, n):
        return pl.ds(TOK // n * ch, TOK // n)

    def upper(ch, n):
        return ch % 2 == 0 if n == 2 else ch // 2 % 2 == 0

    def piece(buf, k, c, at):
        return buf.at[k, c, :, at] if len(buf.shape) == 5 else buf.at[k, c, at]

    def to_mate(name, buf, d, ch, n):
        k = PLACE[d]
        at = rows(ch, n)
        group = (name, "c", d, 2 * ch // n if n == FINE else 0)
        make((name, "c"), group, piece(buf, k, 0, at), piece(buf, k, 1, at), mate).start()

    def gathered(name, buf, d, h=0, at=pl.ds(0, TOK)):
        k = PLACE[d]
        group = (name, "c", d, h)
        make((name, "c"), group, piece(buf, k, 0, at), piece(buf, k, 1, at), mate).wait_recv()

    def hop(name, buf, way, d, ch, n):
        src, dst = (d, d + 1) if way == "u" else ((8 - d) % 8, 7 - d)
        at = rows(ch, n)
        send(
            (name, way, d, ch),
            piece(buf, PLACE[src], 0, at),
            piece(buf, PLACE[dst], 0, at),
            z_up if way == "u" else z_down,
            (name, "z"),
        )

    def gather_first(name, buf, ch, n):
        hop(name, buf, "u", 0, ch, n)
        hop(name, buf, "d", 0, ch, n)
        to_mate(name, buf, 0, ch, n)

    def gather_step(name, buf, d, chs, n):
        for pair in chs:
            for way, ch in zip("ud", pair):
                here = d if way == "u" else 8 - d
                half = (way == "u") == upper(ch, n)
                if d < 4 or half:
                    sent[name, way, d - 1, ch].wait_recv()
                    if d < 3 or (d == 3 and half):
                        hop(name, buf, way, d, ch, n)
                    to_mate(name, buf, here, ch, n)

    def table_step(d):
        def on(way, d, k, to, peer):
            send(("t", way, d), tab.at[k, 0], tab.at[to, 0], peer, ("t", "z"))

        def across(d, k):
            make(("t", "c"), ("t", "c"), tab.at[k, 0], tab.at[k, 1], mate).start()

        if d == 0:
            on("u", 0, 0, PLACE[1], z_up)
            on("d", 0, 0, PLACE[7], z_down)
            across(0, 0)
            return
        sent["t", "u", d - 1].wait_recv()
        k = PLACE[d]
        if d < 4:
            on("u", d, k, PLACE[d + 1], z_up)
        across(d, k)
        if d < 4:
            sent["t", "d", d - 1].wait_recv()
            k = PLACE[8 - d]
            if d < 3:
                on("d", d, k, PLACE[7 - d], z_down)
            across(8 - d, k)

    def tables_there():
        make(("t", "c"), ("t", "c"), tab.at[:, 0], tab.at[:, 1], mate).wait_recv()

    def half(h):
        return pl.ds(0, TOK) if h is None else pl.ds(64 * h, 64)

    def lanes(k, t, h, first):
        both = [tab[k, c, t, first : first + 8] for c in range(2)]
        if h is not None:
            both = [v[:, 64 * h : 64 * h + 64] for v in both]
        return jnp.concatenate(both, axis=1)

    def places(t, h, pos, post):
        masks = []
        for k in range(RING):
            named = lanes(k, t, h, 0)
            for j in range(2):
                hit = named == (2 * home + j).astype(F32)
                masks.append(jnp.sum(jnp.where(hit, 1.0, 0.0), axis=0, keepdims=True))
        mask = jnp.concatenate(masks, axis=0)
        n = mask.shape[1]
        before = lax.broadcasted_iota(jnp.int32, (n, n), 0) < lax.broadcasted_iota(
            jnp.int32, (n, n), 1
        )
        earlier = nn(mask.astype(BF), jnp.where(before, 1.0, 0.0).astype(BF))
        where = jnp.where(mask > 0.5, earlier, -1000.0)
        pos[...] = where
        turned = jnp.transpose(jnp.concatenate([where, jnp.zeros((112, n), F32)], axis=0))
        for k in range(RING):
            post[k] = turned[:, 2 * k : 2 * k + 2]

    def chosen(pos, k):
        slot = lax.broadcasted_iota(jnp.int32, (CAP, pos.shape[1]), 0).astype(F32)
        return [slot == pos[pl.ds(2 * k + j, 1)] for j in range(2)]

    def unit_rows(k):
        return pl.ds(pl.multiple_of(k * CAP, 16), CAP)

    def pos_of(h):
        return pos_full if h is None else pos_half.at[h]

    def pick(h, tokens, dst, k):
        pos = pos_of(h)
        hot = jnp.concatenate([jnp.where(c, 1.0, 0.0) for c in chosen(pos, k)], axis=0).astype(BF)
        got = nn(hot, tokens.reshape(pos.shape[1], D)).astype(BF)
        dst[0, unit_rows(k)] = got[:CAP]
        dst[1, unit_rows(k)] = got[CAP:]

    def pick_scales(t, h, k):
        named = lanes(k, t, h, 0)
        weight = lanes(k, t, h, 8)
        for j, hit in enumerate(chosen(pos_of(h), k)):
            mine = jnp.sum(
                jnp.where(named == (2 * home + j).astype(F32), weight, 0.0), axis=0, keepdims=True
            )
            ws[t + (h or 0), j, unit_rows(k)] = jnp.sum(jnp.where(hit, mine, 0.0), axis=1, keepdims=True)

    def pre(h, j):
        x = xg[j]
        gp[h, j] = nn(x, wg[j])
        up[h, j] = nn(x, wu[j])

    def post_rows(t, h, j, k0, n):
        at = pl.ds(k0 * CAP, n * CAP)
        hidden = nt(gg[j, at], wd[j])
        gate = gp[h, j, at]
        sig = 1.0 / (1.0 + jnp.exp(-gate))
        hs = hidden * sig
        gate_grad = (hs * up[h, j, at] * (1.0 + gate * (1.0 - sig))).astype(BF)
        up_grad = (hs * gate).astype(BF)
        grown = nt(gate_grad, wg[j]) + nt(up_grad, wu[j])
        grown = (grown * ws[t + h, j, at]).astype(BF)
        for i in range(n):
            rw[k0 + i, j * CAP : (j + 1) * CAP] = grown[i * CAP : (i + 1) * CAP]

    def put(t, h, k):
        col = post_full[k] if h is None else post_half[h, k]
        lane = lax.broadcasted_iota(jnp.int32, (col.shape[0], 2 * CAP), 1).astype(F32)
        hot = jnp.logical_or(lane == col[:, 0:1], lane == col[:, 1:2] + float(CAP))
        summed = nn(jnp.where(hot, 1.0, 0.0).astype(BF), rw[k]).astype(BF)
        part[t, k, :, half(h)] = summed.reshape(2, col.shape[0] // 2, D)

    def halved(t, h, d):
        return h if t == 1 else None

    def give_mate(t, h, d):
        k = PLACE[d]
        h = halved(t, h, d)
        at = half(h)
        send((t, "rc", d, h or 0), part.at[t, k, 1, at], l_core.at[t, k, at], mate, (t, "rc"))

    there = set()

    def mate_there(t, h, *ds):
        for d in ds:
            key = (t, "rc", d, halved(t, h, d) or 0)
            if key not in there:
                there.add(key)
                sent[key].wait_recv()

    def give(t, way, d, ch):
        src = part.at[t, PLACE[d], 0, rows(ch, FINE)]
        if way == "d":
            send((t, "rd", d, ch), src, l_down.at[t, d - 1, rows(ch, FINE)], z_down, (t, "rz"))
        else:
            send((t, "ru", d, ch), src, l_up.at[t, 7 - d, rows(ch, FINE)], z_up, (t, "rz"))

    def add_up(t, way, d, ch, arrived):
        k = PLACE[d]
        at = rows(ch, FINE)
        value = part[t, k, 0, at].astype(F32) + l_core[t, k, at].astype(F32)
        if arrived:
            landed = l_down[t, d, at] if way == "d" else l_up[t, 8 - d, at]
            value = value + landed.astype(F32)
        part[t, k, 0, at] = value.astype(BF)

    def far(t, h):
        mate_there(t, h, 4)
        for i in range(2):
            for way, ch in (("d", 4 * h + i), ("u", 4 * h + 2 + i)):
                add_up(t, way, 4, ch, False)
                give(t, way, 4, ch)

    def near(t, h):
        mate_there(t, h, 3, 5)
        for i in range(2):
            for way, d, ch in (("d", 3, 4 * h + 2 + i), ("u", 5, 4 * h + i)):
                add_up(t, way, d, ch, False)
                give(t, way, d, ch)

    def step(t, n, quarter_d, quarter_u):
        mate_there(t, quarter_d // 2, n, 8 - n)
        for i in range(2):
            for way, d, ch in (("d", n, 2 * quarter_d + i), ("u", 8 - n, 2 * quarter_u + i)):
                back = d + 1 if way == "d" else d - 1
                sent[t, "r" + way, back, ch].wait_recv()
                add_up(t, way, d, ch, True)
                give(t, way, d, ch)

    def scatter_last(t, ch, own):
        mate_there(t, ch // 4, 0)
        sent[t, "rd", 1, ch].wait_recv()
        sent[t, "ru", 7, ch].wait_recv()
        at = rows(ch, FINE)
        tot[t, at] = (
            own[at].astype(F32)
            + (part[t, 0, 0, at].astype(F32) + l_core[t, 0, at].astype(F32))
            + (l_down[t, 0, at].astype(F32) + l_up[t, 0, at].astype(F32))
        ).astype(BF)

    def each(body, first=0, last=RING):
        def turn(k, carry):
            body(k)
            return carry

        lax.fori_loop(first, last, turn, 0)

    both = ((0, 0), (1, 1))
    for ch in range(2):
        entered(("a", ch))
        gather_first("a", xg0, ch, 2)
    entered("t")
    table_step(0)
    for d in (1, 2, 3, 4):
        gather_step("a", xg0, d, both, 2)
        table_step(d)
        if d == 3:
            entered("x1")
            for ch in range(2):
                gather_first("x1", x1, ch, 2)
    tables_there()
    places(0, None, pos_full, post_full)
    for h in range(2):
        places(1, h, pos_half.at[h], post_half.at[h])
    for d in range(RING):
        gathered("a", xg0, d)
    gather_step("x1", x1, 1, both, 2)

    def pick0(k):
        pick(None, xg0[k, :, 0], xg, k)
        pick(None, xg0[k, :, 1], gg, k)
        pick_scales(0, None, k)

    each(pick0)
    gather_step("x1", x1, 2, both, 2)
    for w in ("wg", "wu", "wd"):
        entered((w, 0))
    pre(0, 0)
    gather_step("x1", x1, 3, both, 2)
    for u0 in (0, 4):
        post_rows(0, 0, 0, u0, 4)
    gather_step("x1", x1, 4, both, 2)
    for d in range(RING):
        gathered("x1", x1, d)
    entered(("wg", 1))
    entered(("wu", 1))
    pre(0, 1)

    def pick1(h):
        each(lambda k: pick(h, x1[k, :, half(h)], xg, k))

    pick1(0)
    for h in range(2):
        each(lambda k: pick_scales(1, h, k))
    entered(("wd", 1))

    def finish(t, h, ds):
        for d in ds:
            put(t, halved(t, h, d), PLACE[d])
            give_mate(t, h, d)

    post_rows(0, 0, 1, 5, 3)
    finish(0, 0, (4, 3, 5))
    for h in range(2):
        far(0, h)
        near(0, h)
    post_rows(0, 0, 1, 3, 2)
    finish(0, 0, (2, 6))
    post_rows(0, 0, 1, 0, 3)
    finish(0, 0, (1, 7, 0))
    step(0, 3, 0, 1)
    pre(0, 0)
    step(0, 2, 1, 0)
    step(0, 3, 2, 3)
    pre(0, 1)
    step(0, 2, 0, 1)
    step(0, 2, 3, 2)
    pick1(1)
    pre(1, 0)
    step(0, 1, 0, 0)
    step(0, 1, 1, 1)
    step(0, 2, 2, 3)
    pre(1, 1)
    step(0, 1, 3, 2)

    def passing(quarter):
        for ch in (2 * quarter, 2 * quarter + 1):
            scatter_last(0, ch, xg0.at[0, 0, 1])
            at = rows(ch, FINE)
            send(("pass", ch), tot.at[0, at], g1.at[0, 0, at], pass_to, "pass")

    def passed(quarter):
        for ch in (2 * quarter, 2 * quarter + 1):
            sent["pass", ch].wait_recv()
            gather_first("g1", g1, ch, FINE)

    passing(0)
    passing(1)
    step(0, 1, 2, 3)
    passed(0)
    passed(1)
    passing(2)
    passing(3)

    def level(d, h, i):
        up, down = 4 * h + 2 * i, 4 * h + 2 - 2 * i
        gather_step("g1", g1, d, ((up, down), (up + 1, down + 1)), FINE)

    def take(h, ds):
        for d in ds:
            gathered("g1", g1, d, h, half(h))
            pick(h, g1[PLACE[d], :, half(h)], gg, PLACE[d])

    level(1, 0, 0)
    level(1, 0, 1)
    take(0, (0,))
    passed(2)
    passed(3)
    level(2, 0, 0)
    level(2, 0, 1)
    take(0, (1, 7))
    level(1, 1, 0)
    level(1, 1, 1)
    take(0, (2, 6))
    post_rows(1, 0, 0, 0, 5)
    level(3, 0, 0)
    level(3, 0, 1)
    post_rows(1, 0, 1, 0, 5)
    level(2, 1, 0)
    take(0, (3, 5))
    post_rows(1, 0, 0, 5, 2)
    level(2, 1, 1)
    post_rows(1, 0, 1, 5, 2)
    level(4, 0, 0)
    finish(1, 0, (3, 5))
    level(3, 1, 0)
    take(0, (4,))
    post_rows(1, 0, 0, 7, 1)
    level(3, 1, 1)
    near(1, 0)
    post_rows(1, 0, 1, 7, 1)
    finish(1, 0, (4, 2, 6))
    level(4, 1, 0)
    far(1, 0)
    take(1, (3, 5, 4))
    step(1, 2, 1, 0)
    post_rows(1, 1, 0, 5, 3)
    post_rows(1, 1, 1, 5, 3)
    step(1, 3, 0, 1)
    finish(1, 1, (4, 3, 5))
    finish(1, 0, (1, 7, 0))
    far(1, 1)
    step(1, 2, 0, 1)
    near(1, 1)

    def final(quarter):
        for ch in (2 * quarter, 2 * quarter + 1):
            scatter_last(1, ch, g1.at[0, 0])
            at = rows(ch, FINE)
            enter(("fin", ch), [(tot.at[1, at], out_ref.at[at])], out_ref.at[at])

    take(1, (2, 6))
    post_rows(1, 1, 0, 3, 2)
    post_rows(1, 1, 1, 3, 2)
    finish(1, 1, (2, 6))
    step(1, 3, 2, 3)
    step(1, 1, 0, 0)
    take(1, (0, 1, 7))
    step(1, 2, 3, 2)
    post_rows(1, 1, 0, 0, 3)
    step(1, 2, 2, 3)
    step(1, 1, 1, 1)
    post_rows(1, 1, 1, 0, 3)
    finish(1, 1, (1, 7, 0))
    final(0)
    step(1, 1, 2, 2)
    final(1)
    step(1, 1, 3, 3)
    final(2)
    final(3)
    for ch in range(FINE):
        entered(("fin", ch))

    for name, buf in (("a", xg0), ("x1", x1), ("g1", g1), ("t", tab)):
        group = ("t", "c") if name == "t" else (name, "c", 0, 0)
        make((name, "z"), group, buf.at[0:7, 0], buf.at[0:7, 1], z_up).wait_send()
        make((name, "c"), group, buf.at[:, 0], buf.at[:, 1], mate).wait_send()
    for t in range(2):
        make((t, "rz"), (t, "rc", 0, 0), part.at[t, 0:7, 0], part.at[t, 0:7, 0], z_up).wait_send()
        make((t, "rc"), (t, "rc", 0, 0), part.at[t, :, 1], part.at[t, :, 1], mate).wait_send()
    make("pass", ("pass", 0), tot.at[0], tot.at[0], pass_to).wait_send()

    @pl.when(mixed)
    def _():
        for key, whole in ends:
            make(key, key, whole, whole, swap).wait_send()

    assert len(senders) <= SENDERS and len(takers) <= TAKERS, (len(senders), len(takers))

def shards(grad_out, saved_inputs, routes, gate_weights, w_gate, w_up, w_down):
    block = pltpu.VMEM((RING, 2, TOK, D), BF)
    return pl.pallas_call(
        kernel,
        out_shape=jax.ShapeDtypeStruct((TOK, D), BF),
        in_specs=[pl.BlockSpec(memory_space=pl.ANY)] * 7,
        out_specs=pl.BlockSpec(memory_space=pl.ANY),
        scratch_shapes=[
            pltpu.VMEM((RING, 2, 2, TOK, D), BF),
            block, block,
            pltpu.VMEM((RING, 2, 2, 16, TOK), F32),
            pltpu.VMEM((2, D, H), BF),
            pltpu.VMEM((2, D, H), BF),
            pltpu.VMEM((2, H, D), BF),
            pltpu.VMEM((2, RING, 2, TOK, D), BF),
            pltpu.VMEM((2, RING, TOK, D), BF),
            pltpu.VMEM((2, 4, TOK, D), BF),
            pltpu.VMEM((2, 4, TOK, D), BF),
            pltpu.VMEM((2, TOK, D), BF),
            pltpu.VMEM((2, RING * CAP, D), BF),
            pltpu.VMEM((2, RING * CAP, D), BF),
            pltpu.VMEM((2, 2, RING * CAP, H), F32),
            pltpu.VMEM((2, 2, RING * CAP, H), F32),
            pltpu.VMEM((RING, 2 * CAP, D), BF),
            pltpu.VMEM((3, 2, RING * CAP, 1), F32),
            pltpu.VMEM((16, 256), F32),
            pltpu.VMEM((RING, 256, 2), F32),
            pltpu.VMEM((2, 16, 128), F32),
            pltpu.VMEM((2, RING, 128, 2), F32),
            pltpu.VMEM((2, 8, TOK), jnp.int32),
            pltpu.VMEM((2, 16, TOK), F32),
            pltpu.SemaphoreType.DMA((SENDERS,)),
            pltpu.SemaphoreType.DMA((TAKERS,)),
            pltpu.SemaphoreType.DMA((20,)),
        ],
        compiler_params=pltpu.CompilerParams(
            collective_id=0, has_side_effects=True, vmem_limit_bytes=63 << 20
        ),
        name="moe_back",
    )(
        grad_out[0],
        saved_inputs[0],
        jnp.swapaxes(routes[0], 1, 2),
        jnp.swapaxes(gate_weights[0], 1, 2),
        w_gate[0],
        w_up[0],
        w_down[0],
    )[None]


def solution(mesh):
    placed = (
        P("section", "expert", None),
        P("section", None, "expert", None),
        P("section", None, "expert", None),
        P("section", None, "expert", None),
        P("section", "expert", None, None),
        P("section", "expert", None, None),
        P("section", "expert", None, None),
    )
    return jax.shard_map(
        shards, mesh=mesh, in_specs=placed, out_specs=P("section", "expert", None), check_vma=False
    )
```

```python
import jax
import jax.numpy as jnp
from jax import lax
from jax.experimental import pallas as pl
from jax.experimental.pallas import tpu as pltpu
from jax.sharding import PartitionSpec as P

BF = jnp.bfloat16
F32 = jnp.float32
TOK = 128
D = 1024
H = 512
CAP = 80
RING = 8
PLACE = {0: 0, 1: 1, 7: 2, 2: 3, 6: 4, 3: 5, 5: 6, 4: 7}
SENDERS = 31
TAKERS = 152
FINE = 8


def nt(a, b):
    return lax.dot_general(a, b, (((1,), (1,)), ((), ())), preferred_element_type=F32)


def nn(a, b):
    return lax.dot_general(a, b, (((1,), (0,)), ((), ())), preferred_element_type=F32)


def kernel(
    grad_in, saved_in, routes_in, weights_in, wg_in, wu_in, wd_in, out_ref,
    xg0, x1, g1, tab, wg, wu, wd, part, l_core, l_down, l_up, tot,
    xg, gg, gp, up, rw, ws, pos_full, post_full, pos_half, post_half, own_routes, own_table, ssem, rsem, lsem,
):
    s = lax.axis_index("section")
    e = lax.axis_index("expert")
    core = lax.rem(s, 2)
    x_lo = lax.rem(e, 2)
    mixed = core == x_lo
    other_core = s + 1 - 2 * core
    other_x = e + 1 - 2 * x_lo
    z_up = (s, lax.rem(e + 2, 16))
    z_down = (s, lax.rem(e + 14, 16))
    mate = (other_core, e)
    swap = (other_core, other_x)
    pass_to = (lax.rem(s + 16 - 2 * x_lo, 16), other_x)
    pass_from = (lax.rem(s + 2 * (1 - x_lo), 16), other_x)
    home = lax.select(mixed, other_x, e)

    barrier = pltpu.get_barrier_semaphore()
    for peer in (z_up, z_down, mate, swap, pass_to, pass_from):
        pl.semaphore_signal(barrier, inc=1, device_id=peer, device_id_type=pl.DeviceIdType.MESH)

    senders, takers, sent, ends = {}, {}, {}, []

    def number(table, key):
        return table.setdefault(key, len(table))

    def make(batch, group, src, dst, peer):
        if group[0] == 1:
            group = (0,) + group[1:]
        elif group[0] == "x1" and group[1:2] != ("c",) and len(group) == 4:
            group = ("a",) + group[1:]
        elif group[0] == "g1" and group[1] == "c":
            group = ("a",) + group[1:]
        elif group[0] == "g1":
            place = 4 if group[2] == 3 else 3 - group[2]
            group = (0, "r" + group[1], place if group[1] == "d" else 8 - place, group[3])
        return pltpu.make_async_remote_copy(
            src_ref=src, dst_ref=dst,
            send_sem=ssem.at[number(senders, batch)], recv_sem=rsem.at[number(takers, group)],
            device_id=peer, device_id_type=pl.DeviceIdType.MESH,
        )

    def send(key, src, dst, peer, batch):
        sent[key] = make(batch, key, src, dst, peer)
        sent[key].start()

    moves = {}

    def enter(key, pairs, whole):
        i = number(moves, key)

        @pl.when(jnp.logical_not(mixed))
        def _():
            for src, dst in pairs:
                pltpu.make_async_copy(src, dst, lsem.at[i]).start()

        @pl.when(mixed)
        def _():
            for src, dst in pairs:
                make(key, key, src, dst, swap).start()

        ends.append((key, whole))

    def entered(key):
        whole = dict(ends)[key]

        @pl.when(jnp.logical_not(mixed))
        def _():
            pltpu.make_async_copy(whole, whole, lsem.at[moves[key]]).wait()

        @pl.when(mixed)
        def _():
            make(key, key, whole, whole, swap).wait_recv()

    loads = [
        pltpu.make_async_copy(routes_in, own_routes, lsem.at[18]),
        pltpu.make_async_copy(weights_in, own_table.at[:, 8:16], lsem.at[19]),
    ]
    for load in loads:
        load.start()
    pl.semaphore_wait(barrier, 6)
    for ch in range(2):
        at = pl.ds(64 * ch, 64)
        enter(
            ("a", ch),
            [
                (saved_in.at[0, at], xg0.at[0, 0, 0, at]),
                (grad_in.at[at], xg0.at[0, 0, 1, at]),
            ],
            xg0.at[0, 0, :, at],
        )
    for load in loads:
        load.wait()
    own_table[:, 0:8] = own_routes[...].astype(F32)
    enter("t", [(own_table, tab.at[0, 0])], tab.at[0, 0])
    for j in range(2):
        for name, src, dst in (("wg", wg_in, wg), ("wu", wu_in, wu), ("wd", wd_in, wd)):
            enter((name, j), [(src.at[j], dst.at[j])], dst.at[j])
        if j == 0:
            enter("x1", [(saved_in.at[1], x1.at[0, 0])], x1.at[0, 0])

    def rows(ch, n):
        return pl.ds(TOK // n * ch, TOK // n)

    def upper(ch, n):
        return ch % 2 == 0 if n == 2 else ch // 2 % 2 == 0

    def piece(buf, k, c, at):
        return buf.at[k, c, :, at] if len(buf.shape) == 5 else buf.at[k, c, at]

    def to_mate(name, buf, d, ch, n):
        k = PLACE[d]
        at = rows(ch, n)
        group = (name, "c", d, 2 * ch // n if n == FINE else 0)
        make((name, "c"), group, piece(buf, k, 0, at), piece(buf, k, 1, at), mate).start()

    def gathered(name, buf, d, h=0, at=pl.ds(0, TOK)):
        k = PLACE[d]
        group = (name, "c", d, h)
        make((name, "c"), group, piece(buf, k, 0, at), piece(buf, k, 1, at), mate).wait_recv()

    def hop(name, buf, way, d, ch, n):
        src, dst = (d, d + 1) if way == "u" else ((8 - d) % 8, 7 - d)
        at = rows(ch, n)
        send(
            (name, way, d, ch),
            piece(buf, PLACE[src], 0, at),
            piece(buf, PLACE[dst], 0, at),
            z_up if way == "u" else z_down,
            (name, "z"),
        )

    def gather_first(name, buf, ch, n):
        hop(name, buf, "u", 0, ch, n)
        hop(name, buf, "d", 0, ch, n)
        to_mate(name, buf, 0, ch, n)

    def gather_step(name, buf, d, chs, n):
        for pair in chs:
            for way, ch in zip("ud", pair):
                here = d if way == "u" else 8 - d
                half = (way == "u") == upper(ch, n)
                if d < 4 or half:
                    sent[name, way, d - 1, ch].wait_recv()
                    if d < 3 or (d == 3 and half):
                        hop(name, buf, way, d, ch, n)
                    to_mate(name, buf, here, ch, n)

    def table_step(d):
        def on(way, d, k, to, peer):
            send(("t", way, d), tab.at[k, 0], tab.at[to, 0], peer, ("t", "z"))

        def across(d, k):
            make(("t", "c"), ("t", "c"), tab.at[k, 0], tab.at[k, 1], mate).start()

        if d == 0:
            on("u", 0, 0, PLACE[1], z_up)
            on("d", 0, 0, PLACE[7], z_down)
            across(0, 0)
            return
        sent["t", "u", d - 1].wait_recv()
        k = PLACE[d]
        if d < 4:
            on("u", d, k, PLACE[d + 1], z_up)
        across(d, k)
        if d < 4:
            sent["t", "d", d - 1].wait_recv()
            k = PLACE[8 - d]
            if d < 3:
                on("d", d, k, PLACE[7 - d], z_down)
            across(8 - d, k)

    def tables_there():
        make(("t", "c"), ("t", "c"), tab.at[:, 0], tab.at[:, 1], mate).wait_recv()

    def half(h):
        return pl.ds(0, TOK) if h is None else pl.ds(64 * h, 64)

    def lanes(k, t, h, first):
        both = [tab[k, c, t, first : first + 8] for c in range(2)]
        if h is not None:
            both = [v[:, 64 * h : 64 * h + 64] for v in both]
        return jnp.concatenate(both, axis=1)

    def places(t, h, pos, post):
        masks = []
        for k in range(RING):
            named = lanes(k, t, h, 0)
            for j in range(2):
                hit = named == (2 * home + j).astype(F32)
                masks.append(jnp.sum(jnp.where(hit, 1.0, 0.0), axis=0, keepdims=True))
        mask = jnp.concatenate(masks, axis=0)
        n = mask.shape[1]
        before = lax.broadcasted_iota(jnp.int32, (n, n), 0) < lax.broadcasted_iota(
            jnp.int32, (n, n), 1
        )
        earlier = nn(mask.astype(BF), jnp.where(before, 1.0, 0.0).astype(BF))
        where = jnp.where(mask > 0.5, earlier, -1000.0)
        pos[...] = where
        turned = jnp.transpose(jnp.concatenate([where, jnp.zeros((112, n), F32)], axis=0))
        for k in range(RING):
            post[k] = turned[:, 2 * k : 2 * k + 2]

    def chosen(pos, k):
        slot = lax.broadcasted_iota(jnp.int32, (CAP, pos.shape[1]), 0).astype(F32)
        return [slot == pos[pl.ds(2 * k + j, 1)] for j in range(2)]

    def unit_rows(k):
        return pl.ds(pl.multiple_of(k * CAP, 16), CAP)

    def pos_of(h):
        return pos_full if h is None else pos_half.at[h]

    def pick(h, tokens, dst, k):
        pos = pos_of(h)
        hot = jnp.concatenate([jnp.where(c, 1.0, 0.0) for c in chosen(pos, k)], axis=0).astype(BF)
        got = nn(hot, tokens.reshape(pos.shape[1], D)).astype(BF)
        dst[0, unit_rows(k)] = got[:CAP]
        dst[1, unit_rows(k)] = got[CAP:]

    def pick_scales(t, h, k):
        named = lanes(k, t, h, 0)
        weight = lanes(k, t, h, 8)
        for j, hit in enumerate(chosen(pos_of(h), k)):
            mine = jnp.sum(
                jnp.where(named == (2 * home + j).astype(F32), weight, 0.0), axis=0, keepdims=True
            )
            ws[t + (h or 0), j, unit_rows(k)] = jnp.sum(jnp.where(hit, mine, 0.0), axis=1, keepdims=True)

    def pre(h, j):
        x = xg[j]
        gp[h, j] = nn(x, wg[j])
        up[h, j] = nn(x, wu[j])

    def post_rows(t, h, j, k0, n):
        at = pl.ds(k0 * CAP, n * CAP)
        hidden = nt(gg[j, at], wd[j])
        gate = gp[h, j, at]
        sig = 1.0 / (1.0 + jnp.exp(-gate))
        hs = hidden * sig
        gate_grad = (hs * up[h, j, at] * (1.0 + gate * (1.0 - sig))).astype(BF)
        up_grad = (hs * gate).astype(BF)
        grown = nt(gate_grad, wg[j]) + nt(up_grad, wu[j])
        grown = (grown * ws[t + h, j, at]).astype(BF)
        for i in range(n):
            rw[k0 + i, j * CAP : (j + 1) * CAP] = grown[i * CAP : (i + 1) * CAP]

    def put(t, h, k):
        col = post_full[k] if h is None else post_half[h, k]
        lane = lax.broadcasted_iota(jnp.int32, (col.shape[0], 2 * CAP), 1).astype(F32)
        hot = jnp.logical_or(lane == col[:, 0:1], lane == col[:, 1:2] + float(CAP))
        summed = nn(jnp.where(hot, 1.0, 0.0).astype(BF), rw[k]).astype(BF)
        part[t, k, :, half(h)] = summed.reshape(2, col.shape[0] // 2, D)

    def halved(t, h, d):
        return h if t == 1 else None

    def give_mate(t, h, d):
        k = PLACE[d]
        h = halved(t, h, d)
        at = half(h)
        send((t, "rc", d, h or 0), part.at[t, k, 1, at], l_core.at[t, k, at], mate, (t, "rc"))

    there = set()

    def mate_there(t, h, *ds):
        for d in ds:
            key = (t, "rc", d, halved(t, h, d) or 0)
            if key not in there:
                there.add(key)
                sent[key].wait_recv()

    def give(t, way, d, ch):
        src = part.at[t, PLACE[d], 0, rows(ch, FINE)]
        if way == "d":
            send((t, "rd", d, ch), src, l_down.at[t, d - 1, rows(ch, FINE)], z_down, (t, "rz"))
        else:
            send((t, "ru", d, ch), src, l_up.at[t, 7 - d, rows(ch, FINE)], z_up, (t, "rz"))

    def add_up(t, way, d, ch, arrived):
        k = PLACE[d]
        at = rows(ch, FINE)
        value = part[t, k, 0, at].astype(F32) + l_core[t, k, at].astype(F32)
        if arrived:
            landed = l_down[t, d, at] if way == "d" else l_up[t, 8 - d, at]
            value = value + landed.astype(F32)
        part[t, k, 0, at] = value.astype(BF)

    def far(t, h):
        mate_there(t, h, 4)
        for i in range(2):
            for way, ch in (("d", 4 * h + i), ("u", 4 * h + 2 + i)):
                add_up(t, way, 4, ch, False)
                give(t, way, 4, ch)

    def near(t, h):
        mate_there(t, h, 3, 5)
        for i in range(2):
            for way, d, ch in (("d", 3, 4 * h + 2 + i), ("u", 5, 4 * h + i)):
                add_up(t, way, d, ch, False)
                give(t, way, d, ch)

    def step(t, n, quarter_d, quarter_u):
        mate_there(t, quarter_d // 2, n, 8 - n)
        for i in range(2):
            for way, d, ch in (("d", n, 2 * quarter_d + i), ("u", 8 - n, 2 * quarter_u + i)):
                back = d + 1 if way == "d" else d - 1
                sent[t, "r" + way, back, ch].wait_recv()
                add_up(t, way, d, ch, True)
                give(t, way, d, ch)

    def scatter_last(t, ch, own):
        mate_there(t, ch // 4, 0)
        sent[t, "rd", 1, ch].wait_recv()
        sent[t, "ru", 7, ch].wait_recv()
        at = rows(ch, FINE)
        tot[t, at] = (
            own[at].astype(F32)
            + (part[t, 0, 0, at].astype(F32) + l_core[t, 0, at].astype(F32))
            + (l_down[t, 0, at].astype(F32) + l_up[t, 0, at].astype(F32))
        ).astype(BF)

    def each(body, first=0, last=RING):
        def turn(k, carry):
            body(k)
            return carry

        lax.fori_loop(first, last, turn, 0)

    both = ((0, 0), (1, 1))
    for ch in range(2):
        entered(("a", ch))
        gather_first("a", xg0, ch, 2)
    entered("t")
    table_step(0)
    for d in (1, 2, 3, 4):
        gather_step("a", xg0, d, both, 2)
        table_step(d)
        if d == 3:
            entered("x1")
            for ch in range(2):
                gather_first("x1", x1, ch, 2)
    tables_there()
    places(0, None, pos_full, post_full)
    for h in range(2):
        places(1, h, pos_half.at[h], post_half.at[h])
    for d in range(RING):
        gathered("a", xg0, d)
    gather_step("x1", x1, 1, both, 2)

    def pick0(k):
        pick(None, xg0[k, :, 0], xg, k)
        pick(None, xg0[k, :, 1], gg, k)
        pick_scales(0, None, k)

    each(pick0)
    gather_step("x1", x1, 2, both, 2)
    for w in ("wg", "wu", "wd"):
        entered((w, 0))
    pre(0, 0)
    gather_step("x1", x1, 3, both, 2)
    for u0 in (0, 4):
        post_rows(0, 0, 0, u0, 4)
    gather_step("x1", x1, 4, both, 2)
    for d in range(RING):
        gathered("x1", x1, d)
    entered(("wg", 1))
    entered(("wu", 1))
    pre(0, 1)

    def pick1(h):
        each(lambda k: pick(h, x1[k, :, half(h)], xg, k))

    pick1(0)
    for h in range(2):
        each(lambda k: pick_scales(1, h, k))
    entered(("wd", 1))

    def finish(t, h, ds):
        for d in ds:
            put(t, halved(t, h, d), PLACE[d])
            give_mate(t, h, d)

    post_rows(0, 0, 1, 5, 3)
    finish(0, 0, (4, 3, 5))
    for h in range(2):
        far(0, h)
        near(0, h)
    post_rows(0, 0, 1, 3, 2)
    finish(0, 0, (2, 6))
    post_rows(0, 0, 1, 0, 3)
    finish(0, 0, (1, 7, 0))
    step(0, 3, 0, 1)
    pre(0, 0)
    step(0, 2, 1, 0)
    step(0, 3, 2, 3)
    pre(0, 1)
    step(0, 2, 0, 1)
    step(0, 2, 3, 2)
    pick1(1)
    pre(1, 0)
    step(0, 1, 0, 0)
    step(0, 1, 1, 1)
    step(0, 2, 2, 3)
    pre(1, 1)
    step(0, 1, 3, 2)

    def passing(quarter):
        for ch in (2 * quarter, 2 * quarter + 1):
            scatter_last(0, ch, xg0.at[0, 0, 1])
            at = rows(ch, FINE)
            send(("pass", ch), tot.at[0, at], g1.at[0, 0, at], pass_to, "pass")

    def passed(quarter):
        for ch in (2 * quarter, 2 * quarter + 1):
            sent["pass", ch].wait_recv()
            gather_first("g1", g1, ch, FINE)

    passing(0)
    passing(1)
    step(0, 1, 2, 3)
    passed(0)
    passed(1)
    passing(2)
    passing(3)

    def level(d, h, i):
        up, down = 4 * h + 2 * i, 4 * h + 2 - 2 * i
        gather_step("g1", g1, d, ((up, down), (up + 1, down + 1)), FINE)

    def take(h, ds):
        for d in ds:
            gathered("g1", g1, d, h, half(h))
            pick(h, g1[PLACE[d], :, half(h)], gg, PLACE[d])

    level(1, 0, 0)
    level(1, 0, 1)
    take(0, (0,))
    passed(2)
    passed(3)
    level(2, 0, 0)
    level(2, 0, 1)
    take(0, (1, 7))
    level(1, 1, 0)
    level(1, 1, 1)
    take(0, (2, 6))
    post_rows(1, 0, 0, 0, 5)
    level(3, 0, 0)
    level(3, 0, 1)
    post_rows(1, 0, 1, 0, 5)
    level(2, 1, 0)
    take(0, (3, 5))
    post_rows(1, 0, 0, 5, 2)
    level(2, 1, 1)
    post_rows(1, 0, 1, 5, 2)
    level(4, 0, 0)
    finish(1, 0, (3, 5))
    level(3, 1, 0)
    take(0, (4,))
    post_rows(1, 0, 0, 7, 1)
    level(3, 1, 1)
    near(1, 0)
    post_rows(1, 0, 1, 7, 1)
    finish(1, 0, (4, 2, 6))
    level(4, 1, 0)
    far(1, 0)
    take(1, (3, 5, 4))
    step(1, 2, 1, 0)
    post_rows(1, 1, 0, 5, 3)
    post_rows(1, 1, 1, 5, 3)
    step(1, 3, 0, 1)
    finish(1, 1, (4, 3, 5))
    finish(1, 0, (1, 7, 0))
    far(1, 1)
    step(1, 2, 0, 1)
    near(1, 1)

    def final(quarter):
        for ch in (2 * quarter, 2 * quarter + 1):
            scatter_last(1, ch, g1.at[0, 0])
            at = rows(ch, FINE)
            enter(("fin", ch), [(tot.at[1, at], out_ref.at[at])], out_ref.at[at])

    take(1, (2, 6))
    post_rows(1, 1, 0, 3, 2)
    post_rows(1, 1, 1, 3, 2)
    finish(1, 1, (2, 6))
    step(1, 3, 2, 3)
    step(1, 1, 0, 0)
    take(1, (0, 1, 7))
    step(1, 2, 3, 2)
    post_rows(1, 1, 0, 0, 3)
    post_rows(1, 1, 1, 0, 3)
    step(1, 2, 2, 3)
    step(1, 1, 1, 1)
    finish(1, 1, (1, 7, 0))
    final(0)
    step(1, 1, 2, 2)
    final(1)
    step(1, 1, 3, 3)
    final(2)
    final(3)
    for ch in range(FINE):
        entered(("fin", ch))

    for name, buf in (("a", xg0), ("x1", x1), ("g1", g1), ("t", tab)):
        group = ("t", "c") if name == "t" else (name, "c", 0, 0)
        make((name, "z"), group, buf.at[0:7, 0], buf.at[0:7, 1], z_up).wait_send()
        make((name, "c"), group, buf.at[:, 0], buf.at[:, 1], mate).wait_send()
    for t in range(2):
        make((t, "rz"), (t, "rc", 0, 0), part.at[t, 0:7, 0], part.at[t, 0:7, 0], z_up).wait_send()
        make((t, "rc"), (t, "rc", 0, 0), part.at[t, :, 1], part.at[t, :, 1], mate).wait_send()
    make("pass", ("pass", 0), tot.at[0], tot.at[0], pass_to).wait_send()

    @pl.when(mixed)
    def _():
        for key, whole in ends:
            make(key, key, whole, whole, swap).wait_send()

    assert len(senders) <= SENDERS and len(takers) <= TAKERS, (len(senders), len(takers))

def shards(grad_out, saved_inputs, routes, gate_weights, w_gate, w_up, w_down):
    block = pltpu.VMEM((RING, 2, TOK, D), BF)
    return pl.pallas_call(
        kernel,
        out_shape=jax.ShapeDtypeStruct((TOK, D), BF),
        in_specs=[pl.BlockSpec(memory_space=pl.ANY)] * 7,
        out_specs=pl.BlockSpec(memory_space=pl.ANY),
        scratch_shapes=[
            pltpu.VMEM((RING, 2, 2, TOK, D), BF),
            block, block,
            pltpu.VMEM((RING, 2, 2, 16, TOK), F32),
            pltpu.VMEM((2, D, H), BF),
            pltpu.VMEM((2, D, H), BF),
            pltpu.VMEM((2, H, D), BF),
            pltpu.VMEM((2, RING, 2, TOK, D), BF),
            pltpu.VMEM((2, RING, TOK, D), BF),
            pltpu.VMEM((2, 4, TOK, D), BF),
            pltpu.VMEM((2, 4, TOK, D), BF),
            pltpu.VMEM((2, TOK, D), BF),
            pltpu.VMEM((2, RING * CAP, D), BF),
            pltpu.VMEM((2, RING * CAP, D), BF),
            pltpu.VMEM((2, 2, RING * CAP, H), F32),
            pltpu.VMEM((2, 2, RING * CAP, H), F32),
            pltpu.VMEM((RING, 2 * CAP, D), BF),
            pltpu.VMEM((3, 2, RING * CAP, 1), F32),
            pltpu.VMEM((16, 256), F32),
            pltpu.VMEM((RING, 256, 2), F32),
            pltpu.VMEM((2, 16, 128), F32),
            pltpu.VMEM((2, RING, 128, 2), F32),
            pltpu.VMEM((2, 8, TOK), jnp.int32),
            pltpu.VMEM((2, 16, TOK), F32),
            pltpu.SemaphoreType.DMA((SENDERS,)),
            pltpu.SemaphoreType.DMA((TAKERS,)),
            pltpu.SemaphoreType.DMA((20,)),
        ],
        compiler_params=pltpu.CompilerParams(
            collective_id=0, has_side_effects=True, vmem_limit_bytes=63 << 20
        ),
        name="moe_back",
    )(
        grad_out[0],
        saved_inputs[0],
        jnp.swapaxes(routes[0], 1, 2),
        jnp.swapaxes(gate_weights[0], 1, 2),
        w_gate[0],
        w_up[0],
        w_down[0],
    )[None]


def solution(mesh):
    placed = (
        P("section", "expert", None),
        P("section", None, "expert", None),
        P("section", None, "expert", None),
        P("section", None, "expert", None),
        P("section", "expert", None, None),
        P("section", "expert", None, None),
        P("section", "expert", None, None),
    )
    return jax.shard_map(
        shards, mesh=mesh, in_specs=placed, out_specs=P("section", "expert", None), check_vma=False
    )
```
